512 devices in a mesh: section: 8 (over x, core), seq: 64 (over z, y).
Axes of the slice: x: 4, y: 8, z: 8, core: 2. Of those that a mesh axis runs over, the one named last changes fastest.
Arguments:
- stream: bfloat16 [8, 8192, 4096], P('section', 'seq'), may hold values from -200 to 200
- cotangent: bfloat16 [8, 8192, 4096], P('section', 'seq'), may hold values from -24 to 24
- keys: bfloat16 [8, 8192, 512], P('section', 'seq'), may hold values from -30 to 30
- values: bfloat16 [8, 8192, 512], P('section', 'seq'), may hold values from -6 to 6
- gain: float32 [8, 4096], P('section'), may hold values from 0.5 to 2
- rand_blocks: int32 [64, 1], P('seq'), may hold values from 0 to 63, as said below
Outputs:
- stream_grads: bfloat16 [8, 8192, 4096], P('section', 'seq')
- key_grads: bfloat16 [8, 8192, 512], P('section', 'seq')
- value_grads: bfloat16 [8, 8192, 512], P('section', 'seq')
The draws below stay inside these ranges and needn't reach their ends.
Inputs may be any that keep to these rules, and one draw needn't show every extreme that they name: `rand_blocks`: row d names one block, of the form d xor 2**b with b >= 1; every row d = 2**b with b >= 1 names block 0.
All inputs are finite; a program needn't handle non-finite values.
Results may differ from the reference program's by a relative error of at most 0.012.
The reference program's roundings to bfloat16 on the way count: a program that leaves them out, or rounds other values in their place, can miss the bound.
Values may be sent and summed in bfloat16 or wider, within the bound.
A program may use at most 128 MiB of HBM per device.

```python
import math
import jax
import jax.numpy as jnp
from jax import lax

QH = 32
HD = 128
BLOCK = 128
RAND = 1
SECTIONS = 8
TOKENS = 8192
NBLK = 64
SLOTS = 5
WIDTH = 4096
KVW = 512


def draw_stream(key, part):
    shape = (SECTIONS, TOKENS, WIDTH)
    return jnp.clip(jax.random.normal(jax.random.fold_in(key, 23), shape), -6.0, 6.0).astype(jnp.bfloat16)


def draw_keys(key, part):
    shape = (SECTIONS, TOKENS, KVW)
    return jnp.clip(2.0 * jax.random.normal(jax.random.fold_in(key, 33), shape), -8.0, 8.0).astype(jnp.bfloat16)


def draw_rand_blocks(key, part):
    block_count = TOKENS // BLOCK
    bit_count = block_count.bit_length() - 1
    row_index = jnp.arange(block_count, dtype=jnp.int32)[:, None]
    bit_values = jnp.arange(1, bit_count, dtype=jnp.int32)[None, :]
    partner = jnp.bitwise_xor(row_index, jnp.left_shift(jnp.int32(1), bit_values))
    noise_draw = jax.random.randint(jax.random.fold_in(key, 41), (block_count, bit_count - 1), 0, 1 << 20)
    ranking = noise_draw * 64 + bit_values
    ranking = jnp.where(partner == 0, 1 << 28, ranking)
    ranked_values, picked = lax.top_k(ranking, RAND)
    chosen_bits = picked.astype(jnp.int32) + 1
    return jnp.bitwise_xor(row_index, jnp.left_shift(jnp.int32(1), chosen_bits)).astype(jnp.int32)


def block_levels(key, extent, split, low, high):
    def one(dim, shards_of):
        steps = jax.random.uniform(jax.random.fold_in(jax.random.fold_in(key, 6), dim), (shards_of,), jnp.float32, low / len(split), high / len(split))
        return jnp.repeat(jnp.exp(steps), extent[dim] // shards_of).reshape((-1,) + (1,) * (len(extent) - dim - 1))

    factor_of = one(*split[0])
    for cut in split[1:]:
        factor_of = factor_of * one(*cut)
    return factor_of


def scatter_about(rng, shape, spread, bound, shards=(), kind=jnp.bfloat16):
    drawn = jax.random.normal(rng, shape, jnp.float32) * spread
    if len(shards) > 0:
        drawn = block_levels(rng, shape, shards, -0.22, 0.18) * drawn
    return jnp.clip(drawn, min=-bound, max=bound).astype(kind)


def setup_inputs(seed: int = 0) -> dict:
    key_list = jax.random.split(jax.random.key(seed), 7)
    stream = draw_stream(jax.random.fold_in(key_list[6], 71), 0)
    cotangent = scatter_about(key_list[1], (SECTIONS, TOKENS, WIDTH), 4.0, 24.0, ((0, 8), (1, 64)))
    keys = draw_keys(jax.random.fold_in(key_list[6], 71), 0)
    values = scatter_about(key_list[3], (SECTIONS, TOKENS, KVW), 1.0, 6.0, ((0, 8), (1, 64)))
    gain = jnp.clip(jnp.exp(math.log(2.0) - 1.3862944 * jax.random.uniform(key_list[4], (SECTIONS, WIDTH), jnp.float32) ** block_levels(key_list[4], (SECTIONS, WIDTH), ((0, 8),), -0.2, 0.2)), 0.5, 2.0)
    rand_blocks = draw_rand_blocks(jax.random.fold_in(key_list[6], 71), 0)
    return dict(stream=stream, cotangent=cotangent, keys=keys, values=values, gain=gain, rand_blocks=rand_blocks)


def rounded(array):
    return lax.optimization_barrier(array.astype(jnp.bfloat16)).astype(jnp.float32)

def group_terms(queries, slot_keys, slot_values, slot_valid, upstream):
    row_count = queries.shape[0]
    head_dim = slot_keys.shape[1]
    head_count = queries.shape[1] // head_dim
    factor = head_dim ** (-0.5)
    best = lax.Precision.HIGHEST
    query_heads = queries.astype(jnp.float32).reshape(row_count, head_count, head_dim)
    grad_heads = upstream.astype(jnp.float32).reshape(row_count, head_count, head_dim)
    key_rows = slot_keys.astype(jnp.float32)
    value_rows = slot_values.astype(jnp.float32)
    scores = jnp.einsum('qhd,kd->hqk', query_heads, key_rows, precision=best) * factor
    scores = jnp.where(slot_valid[None, None, :], scores, -1e+30)
    row_peak = lax.optimization_barrier(jnp.max(scores, axis=2, keepdims=True))
    raised = jnp.exp(scores - row_peak)
    weights = raised / lax.optimization_barrier(jnp.sum(raised, axis=2, keepdims=True))
    weights_low = rounded(weights)
    grad_weights = jnp.einsum('qhd,kd->hqk', grad_heads, value_rows, precision=best)
    centred = grad_weights - lax.optimization_barrier(jnp.sum(weights * grad_weights, axis=2, keepdims=True))
    grad_low = rounded(weights * centred * factor)
    grad_query = jnp.einsum('hqk,kd->qhd', grad_low, key_rows, precision=best)
    grad_keys = jnp.einsum('hqk,qhd->kd', grad_low, query_heads, precision=best)
    grad_values = jnp.einsum('hqk,qhd->kd', weights_low, grad_heads, precision=best)
    return (grad_query.reshape(row_count, head_count * head_dim), grad_keys, grad_values)

def section_terms(hidden, upstream, key_rows, value_rows, gain_row, rand_blocks):
    own = jnp.concatenate([key_rows, value_rows], axis=1).reshape(NBLK, BLOCK, 2 * KVW)
    hidden_wide = hidden.astype(jnp.float32)
    inverse = lax.rsqrt(lax.optimization_barrier(jnp.mean(hidden_wide * hidden_wide, axis=1, keepdims=True)) + 1e-05)
    normed = hidden_wide * inverse
    queries = (normed * gain_row).astype(jnp.bfloat16)
    groups = KVW // HD
    query_cols = QH * HD // groups

    def per_block(index):
        empty = jnp.zeros((BLOCK, 2 * KVW), jnp.bfloat16)
        lower = jnp.maximum(index - 1, 0).astype(jnp.int32)
        upper = jnp.minimum(index + 1, NBLK - 1).astype(jnp.int32)
        parts = [jnp.where(index > 0, own[lower], empty), own[index], jnp.where(index < NBLK - 1, own[upper], empty), own[0]]
        for slot_index in range(RAND):
            parts.append(own[rand_blocks[index, slot_index].astype(jnp.int32)])
        slots = jnp.concatenate(parts, axis=0)
        flags = jnp.stack([index > 0, index >= 0, index < NBLK - 1, index > 0] + [index >= 0] * RAND)
        slot_valid = jnp.repeat(flags, BLOCK)
        start = (index * BLOCK).astype(jnp.int32)
        block_queries = lax.dynamic_slice_in_dim(queries, start, BLOCK, 0)
        block_upstream = lax.dynamic_slice_in_dim(upstream, start, BLOCK, 0)
        query_parts = []
        key_parts = []
        value_parts = []
        for group in range(groups):
            grad_query, grad_keys, grad_values = group_terms(block_queries[:, group * query_cols:(group + 1) * query_cols], slots[:, group * HD:(group + 1) * HD], slots[:, KVW + group * HD:KVW + (group + 1) * HD], slot_valid, block_upstream[:, group * query_cols:(group + 1) * query_cols])
            query_parts.append(grad_query)
            key_parts.append(grad_keys)
            value_parts.append(grad_values)
        grad_slots = jnp.concatenate(key_parts + value_parts, axis=1)
        return (jnp.concatenate(query_parts, axis=1), grad_slots)
    grad_query, grad_slots = lax.map(per_block, jnp.arange(NBLK, dtype=jnp.int32))
    grad_query = grad_query.reshape(TOKENS, QH * HD)
    grad_normed = grad_query * gain_row
    grad_hidden = inverse * (grad_normed - normed * lax.optimization_barrier(jnp.mean(grad_normed * normed, axis=1, keepdims=True)))
    handed = (upstream.astype(jnp.float32) + grad_hidden).astype(jnp.bfloat16)
    terms = grad_slots.reshape(NBLK, SLOTS, BLOCK, 2 * KVW)
    zero_block = jnp.zeros((1, BLOCK, 2 * KVW), jnp.float32)
    from_next = jnp.concatenate([rounded(terms[1:, 0]), zero_block], axis=0)
    from_prev = jnp.concatenate([zero_block, rounded(terms[:-1, 2])], axis=0)
    totals = terms[:, 1] + from_prev + from_next
    random_terms = rounded(terms[:, 4:]).reshape(NBLK * RAND, BLOCK, 2 * KVW)
    totals = totals.at[rand_blocks.reshape(-1).astype(jnp.int32)].add(random_terms)
    totals = totals.at[0].add(lax.optimization_barrier(jnp.sum(terms[:, 3], axis=0)))
    totals = totals.astype(jnp.bfloat16).reshape(TOKENS, 2 * KVW)
    return (handed, totals[:, :KVW], totals[:, KVW:])

def reference(stream, cotangent, keys, values, gain, rand_blocks):

    def per_section(items):
        return section_terms(items[0], items[1], items[2], items[3], items[4], rand_blocks)
    handed, key_grads, value_grads = lax.map(per_section, (stream, cotangent, keys, values, gain))
    return (jnp.roll(handed, -1, axis=0), key_grads, value_grads)
```

```python
import math

import jax
import jax.numpy as jnp
from jax import lax
from jax.experimental import pallas as pl
from jax.experimental.pallas import tpu as pltpu
from jax.sharding import PartitionSpec as P

MESH = pl.DeviceIdType.MESH
HD = 128
ROWS = 128
NEG = -1e30
F32 = jnp.float32
BF16 = jnp.bfloat16
SIDE = 8
DIRS = 4
PAR = (0, 1, 0, 1)


def dot(a, b, dims):
    return lax.dot_general(a, b, (dims, ((), ())), preferred_element_type=F32)


def kernel(
    heads,
    groups,
    gain,
    rand,
    stream,
    cotangent,
    keys,
    values,
    stream_out,
    key_out,
    value_out,
    hidden,
    upstream,
    queries,
    grad_query,
    handed,
    blocks,
    corner,
    halo,
    slot_keys,
    slot_values,
    terms,
    far_out,
    far_in,
    far_in2,
    mid_out,
    mid_in,
    near_out,
    near_in,
    edge_out,
    edge_in,
    global_out,
    global_in,
    column_sum,
    column_out,
    row_in,
    row_out,
    last_in,
    local_sem,
    kv_send,
    kv_recv,
    halo_send,
    halo_recv,
    corner_send,
    corner_recv,
    ret_send,
    ret_recv,
    edge_sem,
    global_send,
    global_recv,
    row_send,
    row_recv,
    last_send,
    last_recv,
    handed_sem,
):
    device = lax.axis_index("seq")
    section = lax.axis_index("section")
    sections = lax.axis_size("section")
    z, y = device // SIDE, device % SIDE
    wanted = rand[0, 0]
    pieces = 2 * groups
    per_group = heads // groups
    factor = HD ** (-0.5)

    def at(direction, distance):
        if direction == 0:
            return z * SIDE + (y + distance) % SIDE
        if direction == 1:
            return z * SIDE + (y + SIDE - distance) % SIDE
        if direction == 2:
            return ((z + distance) % SIDE) * SIDE + y
        return ((z + SIDE - distance) % SIDE) * SIDE + y

    def remote(src, dst, send, recv, to):
        return pltpu.make_async_remote_copy(
            src_ref=src,
            dst_ref=dst,
            send_sem=send,
            recv_sem=recv,
            device_id={"seq": to},
            device_id_type=MESH,
        )

    own = []
    for g in range(groups):
        columns = pl.ds(g * HD, HD)
        own.append(pltpu.make_async_copy(keys.at[0, :, columns], blocks.at[0, 2 * g], local_sem.at[2 * g]))
        own.append(
            pltpu.make_async_copy(values.at[0, :, columns], blocks.at[0, 2 * g + 1], local_sem.at[2 * g + 1])
        )
    for copy in own:
        copy.start()
    load_hidden = pltpu.make_async_copy(stream.at[0], hidden, local_sem.at[pieces])
    load_upstream = pltpu.make_async_copy(cotangent.at[0], upstream, local_sem.at[pieces + 1])
    load_hidden.start()
    load_upstream.start()

    barrier = pltpu.get_barrier_semaphore()

    def greet(k, carry):
        pl.semaphore_signal(barrier, inc=1, device_id={"seq": at(0, k)}, device_id_type=MESH)
        pl.semaphore_signal(barrier, inc=1, device_id={"seq": at(2, k)}, device_id_type=MESH)
        return carry

    lax.fori_loop(1, SIDE, greet, 0)
    before = (section + sections - 1) % sections
    after = (section + 1) % sections
    pl.semaphore_signal(barrier, inc=1, device_id={"section": before}, device_id_type=MESH)
    pl.semaphore_signal(barrier, inc=1, device_id={"section": after}, device_id_type=MESH)
    for copy in own:
        copy.wait()
    pl.semaphore_wait(barrier, 2 * (SIDE - 1) + 2)

    def corner_copy(stage, piece, to, index):
        src = blocks.at[0, piece] if stage == 0 else corner.at[piece]
        return remote(src, corner.at[piece], corner_send.at[stage, index], corner_recv.at[piece], to)

    @pl.when(device == 0)
    def _():
        corner[0] = blocks[0, 0]

        def scatter(p, carry):
            corner_copy(0, p, p * SIDE, p).start()
            return carry

        lax.fori_loop(1, SIDE, scatter, 0)

    def slot(direction, step):
        return (step, SIDE - step, SIDE + step, 2 * SIDE - step)[direction]

    def kv(direction, step, g):
        part = pl.ds(2 * g, 2) if step <= 2 else pl.ds(2 * g + PAR[direction], 1)
        src = blocks.at[0 if step == 1 else slot(direction, step - 1), part]
        return remote(
            src,
            blocks.at[slot(direction, step), part],
            kv_send.at[direction, step - 1, g],
            kv_recv.at[direction, step - 1, g],
            at(direction, 1),
        )

    def first(g, carry):
        for direction in range(DIRS):
            kv(direction, 1, g).start()
        return carry

    lax.fori_loop(0, groups, first, 0)

    load_hidden.wait()

    def square(h, total):
        x = hidden[:, pl.ds(pl.multiple_of(h * HD, HD), HD)].astype(F32)
        return total + x * x

    squares = lax.fori_loop(0, heads, square, jnp.zeros((ROWS, HD), F32))
    inverse = lax.rsqrt(jnp.sum(squares, axis=1, keepdims=True) / (heads * HD) + 1e-05)

    def query(h, carry):
        columns = pl.ds(pl.multiple_of(h * HD, HD), HD)
        normed = hidden[:, columns].astype(F32) * inverse
        queries[:, columns] = (normed * gain[:, columns]).astype(BF16)
        return carry

    lax.fori_loop(0, heads, query, 0)

    def halo_copy(g, source, to):
        part = pl.ds(2 * g, 2)
        return remote(blocks.at[source, part], halo.at[part], halo_send.at[g], halo_recv.at[g], to)

    def second(g, carry):
        for direction in (2, 3, 0, 1):
            kv(direction, 1, g).wait_recv()
            kv(direction, 2, g).start()

        @pl.when(y == SIDE - 1)
        def _():
            halo_copy(g, SIDE + 1, z * SIDE).start()

        @pl.when(y == 0)
        def _():
            halo_copy(g, 2 * SIDE - 1, z * SIDE + SIDE - 1).start()

        return carry

    lax.fori_loop(0, groups, second, 0)

    @pl.when(y == 0)
    def _():
        @pl.when(z != 0)
        def _():
            corner_copy(1, z, device, 0).wait_recv()

        def spread(k, carry):
            corner_copy(1, z, at(0, k), k).start()
            return carry

        lax.fori_loop(1, SIDE, spread, 0)

    def onward(step):
        def body(g, carry):
            for direction in range(DIRS):
                kv(direction, step - 1, g).wait_recv()
                kv(direction, step, g).start()
            return carry

        lax.fori_loop(0, groups, body, 0)

    onward(3)

    @pl.when(y != 0)
    def _():
        corner_copy(2, z, device, 0).wait_recv()

    def column(k, carry):
        corner_copy(2, z, at(2, k), k).start()
        return carry

    lax.fori_loop(1, SIDE, column, 0)

    onward(4)

    def collect(g, carry):
        for direction in range(DIRS):
            kv(direction, 4, g).wait_recv()

        @pl.when((y == 0) | (y == SIDE - 1))
        def _():
            halo_copy(g, 0, device).wait_recv()

        return carry

    lax.fori_loop(0, groups, collect, 0)

    def collect_corner(k, carry):
        corner_copy(2, (z + k) % SIDE, device, 0).wait_recv()
        return carry

    lax.fori_loop(1, SIDE, collect_corner, 0)

    wanted_z, wanted_y = wanted // SIDE, wanted % SIDE
    picked = jnp.where(
        wanted_z == z, (y + SIDE - wanted_y) % SIDE, SIDE + (z + SIDE - wanted_z) % SIDE
    )

    def assemble(p, carry):
        for kv_index, target in ((0, slot_keys), (1, slot_values)):
            piece = 2 * p + kv_index
            target[p, pl.ds(0, ROWS)] = jnp.where(y == 0, halo[piece], blocks[1, piece])
            target[p, pl.ds(ROWS, ROWS)] = blocks[0, piece]
            target[p, pl.ds(2 * ROWS, ROWS)] = jnp.where(
                y == SIDE - 1, halo[piece], blocks[SIDE - 1, piece]
            )
            target[p, pl.ds(3 * ROWS, ROWS)] = corner[piece]
            target[p, pl.ds(4 * ROWS, ROWS)] = blocks[picked, piece]
        return carry

    lax.fori_loop(0, groups, assemble, 0)
    terms[...] = jnp.zeros_like(terms)

    load_upstream.wait()

    no_before = jnp.where(device == 0, NEG, 0.0).astype(F32)
    no_after = jnp.where(device == SIDE * SIDE - 1, NEG, 0.0).astype(F32)
    bias = (no_before, None, no_after, no_before, None)
    scale = factor * math.log2(math.e)

    def unit(u, carry):
        g = u // (per_group // 2)
        left = pl.ds(pl.multiple_of(2 * u * HD, HD), HD)
        right = pl.ds(pl.multiple_of(2 * u * HD + HD, HD), HD)
        q = jnp.concatenate([queries[:, left], queries[:, right]], axis=0)
        do = jnp.concatenate([upstream[:, left], upstream[:, right]], axis=0)
        k, v = slot_keys[g], slot_values[g]
        raw = dot(k, q, ((1,), (1,)))
        grad_weights = dot(v, do, ((1,), (1,)))
        scores = []
        for i in range(5):
            part = raw[i * ROWS : (i + 1) * ROWS] * scale
            scores.append(part if bias[i] is None else part + bias[i])
        scores = jnp.concatenate(scores, axis=0)
        peak = jnp.max(scores, axis=0, keepdims=True)
        raised = jnp.exp2(scores - peak)
        weights = raised * (1.0 / jnp.sum(raised, axis=0, keepdims=True))
        row_dot = jnp.sum(weights * grad_weights, axis=0, keepdims=True)
        grad_low = (weights * (grad_weights - row_dot) * factor).astype(BF16)
        weights_low = weights.astype(BF16)
        terms[2 * g] += dot(grad_low, q, ((1,), (0,)))
        terms[2 * g + 1] += dot(weights_low, do, ((1,), (0,)))
        back = dot(grad_low, k, ((0,), (0,)))
        grad_query[:, left] = back[:ROWS]
        grad_query[:, right] = back[ROWS:]
        return carry

    lax.fori_loop(0, heads // 2, unit, 0)

    def mark(to):
        return jnp.where(wanted == to, 1.0, 0.0).astype(F32)

    before_rows, own_rows, after_rows, global_rows, random_rows = (
        pl.ds(i * ROWS, ROWS) for i in range(5)
    )

    def ret(direction, step, g):
        pair = {4: (far_out, far_in), 3: (far_in, far_in2), 2: (mid_out, mid_in), 1: (near_out, near_in)}
        src, dst = pair[step]
        return remote(
            src.at[direction, g],
            dst.at[direction, g],
            ret_send.at[direction, step - 1, g],
            ret_recv.at[direction, step - 1, g],
            at(direction, 1),
        )

    def global_copy(piece, index):
        return remote(
            global_out.at[piece],
            global_in.at[z],
            global_send.at[index],
            global_recv.at[z],
            piece * SIDE + y,
        )

    def edge_copy(to):
        return remote(edge_out, edge_in, edge_sem.at[0], edge_sem.at[1], to)

    def to_bf16(p, carry):
        global_out[p] = terms[p, global_rows].astype(BF16)
        return carry

    lax.fori_loop(0, pieces, to_bf16, 0)

    def send_global(k, carry):
        global_copy((z + k) % SIDE, k).start()
        return carry

    lax.fori_loop(1, SIDE, send_global, 0)

    def send_far(g, carry):
        for direction in range(DIRS):
            random = terms[2 * g + PAR[direction], random_rows]
            far_out[direction, g] = (random * mark(at(direction, 4))).astype(BF16)
            ret(direction, 4, g).start()
        return carry

    lax.fori_loop(0, groups, send_far, 0)

    @pl.when(y == SIDE - 1)
    def _():
        def fill(p, carry):
            edge_out[p] = terms[p, after_rows].astype(BF16)
            return carry

        lax.fori_loop(0, pieces, fill, 0)
        edge_copy(at(2, 1)).start()

    @pl.when(y == 0)
    def _():
        def fill(p, carry):
            edge_out[p] = terms[p, before_rows].astype(BF16)
            return carry

        lax.fori_loop(0, pieces, fill, 0)
        edge_copy(at(3, 1)).start()

    def product(h, total):
        columns = pl.ds(pl.multiple_of(h * HD, HD), HD)
        normed = hidden[:, columns].astype(F32) * inverse
        return total + grad_query[:, columns] * gain[:, columns] * normed

    products = lax.fori_loop(0, heads, product, jnp.zeros((ROWS, HD), F32))
    mean = jnp.sum(products, axis=1, keepdims=True) / (heads * HD)

    def hand(h, carry):
        columns = pl.ds(pl.multiple_of(h * HD, HD), HD)
        normed = hidden[:, columns].astype(F32) * inverse
        grad_norm = grad_query[:, columns] * gain[:, columns]
        grad = inverse * (grad_norm - normed * mean)
        handed[:, columns] = (upstream[:, columns].astype(F32) + grad).astype(BF16)
        return carry

    lax.fori_loop(0, heads, hand, 0)
    hand_over = pltpu.make_async_remote_copy(
        src_ref=handed,
        dst_ref=stream_out.at[0],
        send_sem=handed_sem.at[0],
        recv_sem=handed_sem.at[1],
        device_id={"section": before},
        device_id_type=MESH,
    )
    hand_over.start()

    def pass_far(g, carry):
        for direction in range(DIRS):
            ret(direction, 4, g).wait_recv()
            ret(direction, 3, g).start()
        return carry

    lax.fori_loop(0, groups, pass_far, 0)

    def add_column(k, total):
        source = (z + k) % SIDE
        remote(
            global_out.at[0], global_in.at[source], global_send.at[0], global_recv.at[source], device
        ).wait_recv()
        return total + global_in[source].astype(F32)

    column_sum[...] = lax.fori_loop(1, SIDE, add_column, terms[z, global_rows])

    def row_copy(source, to):
        return remote(column_out, row_in.at[source], row_send.at[0], row_recv.at[source], to)

    @pl.when(y != 0)
    def _():
        column_out[...] = column_sum[...].astype(BF16)
        row_copy(y, z * SIDE).start()

    def send_mid(g, carry):
        for direction in range(DIRS):
            ret(direction, 3, g).wait_recv()
            here = mark(at(direction, 2))
            half = PAR[direction]
            mid_out[direction, g, half] = (
                terms[2 * g + half, random_rows] * here + far_in2[direction, g].astype(F32)
            ).astype(BF16)
            mid_out[direction, g, 1 - half] = (terms[2 * g + 1 - half, random_rows] * here).astype(BF16)
            ret(direction, 2, g).start()
        return carry

    lax.fori_loop(0, groups, send_mid, 0)

    def last_copy(source, to):
        return remote(row_out, last_in.at[source], last_send.at[0], last_recv.at[source], to)

    @pl.when(y == 0)
    def _():
        def add_row(k, total):
            row_copy(k, device).wait_recv()
            return total + row_in[k].astype(F32)

        column_sum[...] = lax.fori_loop(1, SIDE, add_row, column_sum[...])

        @pl.when(z != 0)
        def _():
            row_out[...] = column_sum[...].astype(BF16)
            last_copy(z, 0).start()

    @pl.when((y == 0) | (y == SIDE - 1))
    def _():
        edge_copy(device).wait_recv()

    def send_near(g, carry):
        for direction in range(DIRS):
            ret(direction, 2, g).wait_recv()
            for kv_index in range(2):
                p = 2 * g + kv_index
                passed = mid_in[direction, g, kv_index].astype(F32)
                if direction == 0:
                    added = jnp.where(
                        y == SIDE - 1,
                        edge_in[p].astype(F32),
                        terms[p, after_rows].astype(BF16).astype(F32),
                    )
                elif direction == 1:
                    added = jnp.where(
                        y == 0,
                        edge_in[p].astype(F32),
                        terms[p, before_rows].astype(BF16).astype(F32),
                    )
                else:
                    added = terms[p, random_rows] * mark(at(direction, 1))
                near_out[direction, g, kv_index] = (passed + added).astype(BF16)
            ret(direction, 1, g).start()
        return carry

    lax.fori_loop(0, groups, send_near, 0)

    @pl.when(device == 0)
    def _():
        def take(p, carry):
            last_copy(p, device).wait_recv()
            terms[p, own_rows] += last_in[p].astype(F32)
            return carry

        lax.fori_loop(1, SIDE, take, 0)
        terms[0, own_rows] += column_sum[...]

    for g in range(groups):
        for direction in range(DIRS):
            ret(direction, 1, g).wait_recv()
        for kv_index, out in ((0, key_out), (1, value_out)):
            total = terms[2 * g + kv_index, own_rows]
            for direction in range(DIRS):
                total = total + near_in[direction, g, kv_index].astype(F32)
            out[0, :, pl.ds(g * HD, HD)] = total.astype(BF16)

    def sent(g, carry):
        for direction in range(DIRS):
            for step in (1, 2, 3, 4):
                kv(direction, step, g).wait_send()
                ret(direction, step, g).wait_send()

        @pl.when((y == 0) | (y == SIDE - 1))
        def _():
            halo_copy(g, 0, device).wait_send()

        return carry

    lax.fori_loop(0, groups, sent, 0)

    def sent_pieces(k, carry):
        corner_copy(2, 0, device, k).wait_send()
        global_copy(0, k).wait_send()
        return carry

    lax.fori_loop(1, SIDE, sent_pieces, 0)

    @pl.when(y == 0)
    def _():
        def sent_rows(k, carry):
            corner_copy(1, 0, device, k).wait_send()
            return carry

        lax.fori_loop(1, SIDE, sent_rows, 0)

        @pl.when(z == 0)
        def _():
            def sent_corner(k, carry):
                corner_copy(0, 0, device, k).wait_send()
                return carry

            lax.fori_loop(1, SIDE, sent_corner, 0)

        @pl.when(z != 0)
        def _():
            last_copy(z, 0).wait_send()

    @pl.when(y != 0)
    def _():
        row_copy(y, z * SIDE).wait_send()

    @pl.when((y == 0) | (y == SIDE - 1))
    def _():
        edge_copy(device).wait_send()

    hand_over.wait()


def solution(mesh):
    def on_device(stream, cotangent, keys, values, gain, rand_blocks):
        heads = stream.shape[2] // HD
        groups = keys.shape[2] // HD
        pieces = 2 * groups
        block = (ROWS, HD)
        vmem = pl.BlockSpec(memory_space=pltpu.VMEM)
        hbm = pl.BlockSpec(memory_space=pl.ANY)
        dma = pltpu.SemaphoreType.DMA

        def bf16(*shape):
            return pltpu.VMEM(shape, BF16)

        def f32(*shape):
            return pltpu.VMEM(shape, F32)

        def body(*refs):
            kernel(heads, groups, *refs)

        return pl.pallas_call(
            body,
            name="relay",
            out_shape=(
                jax.ShapeDtypeStruct(stream.shape, BF16),
                jax.ShapeDtypeStruct(keys.shape, BF16),
                jax.ShapeDtypeStruct(values.shape, BF16),
            ),
            in_specs=[vmem, pl.BlockSpec(memory_space=pltpu.SMEM), hbm, hbm, hbm, hbm],
            out_specs=(hbm, vmem, vmem),
            scratch_shapes=[
                bf16(ROWS, heads * HD),
                bf16(ROWS, heads * HD),
                bf16(ROWS, heads * HD),
                f32(ROWS, heads * HD),
                bf16(ROWS, heads * HD),
                bf16(2 * SIDE, pieces, *block),
                bf16(pieces, *block),
                bf16(pieces, *block),
                bf16(groups, 5 * ROWS, HD),
                bf16(groups, 5 * ROWS, HD),
                f32(pieces, 5 * ROWS, HD),
                bf16(DIRS, groups, *block),
                bf16(DIRS, groups, *block),
                bf16(DIRS, groups, *block),
                bf16(DIRS, groups, 2, *block),
                bf16(DIRS, groups, 2, *block),
                bf16(DIRS, groups, 2, *block),
                bf16(DIRS, groups, 2, *block),
                bf16(pieces, *block),
                bf16(pieces, *block),
                bf16(pieces, *block),
                bf16(SIDE, *block),
                f32(*block),
                bf16(*block),
                bf16(SIDE, *block),
                bf16(*block),
                bf16(SIDE, *block),
                dma((pieces + 2,)),
                dma((DIRS, 4, groups)),
                dma((DIRS, 4, groups)),
                dma((groups,)),
                dma((groups,)),
                dma((3, SIDE)),
                dma((pieces,)),
                dma((DIRS, 4, groups)),
                dma((DIRS, 4, groups)),
                dma((2,)),
                dma((SIDE,)),
                dma((SIDE,)),
                dma((1,)),
                dma((SIDE,)),
                dma((1,)),
                dma((SIDE,)),
                dma((2,)),
            ],
            compiler_params=pltpu.CompilerParams(
                collective_id=0, has_side_effects=True, vmem_limit_bytes=48 * 1024 * 1024
            ),
        )(gain, rand_blocks, stream, cotangent, keys, values)

    return jax.shard_map(
        on_device,
        mesh=mesh,
        in_specs=(
            P("section", "seq", None),
            P("section", "seq", None),
            P("section", "seq", None),
            P("section", "seq", None),
            P("section", None),
            P("seq", None),
        ),
        out_specs=(P("section", "seq", None), P("section", "seq", None), P("section", "seq", None)),
        check_vma=False,
    )
```

```python
import math

import jax
import jax.numpy as jnp
from jax import lax
from jax.experimental import pallas as pl
from jax.experimental.pallas import tpu as pltpu
from jax.sharding import PartitionSpec as P

MESH = pl.DeviceIdType.MESH
HD = 128
ROWS = 128
HALF = ROWS // 2
NEG = -1e30
F32 = jnp.float32
BF16 = jnp.bfloat16
SIDE = 8
DIRS = 4
PAR = (0, 1, 0, 1)


def dot(a, b, dims):
    return lax.dot_general(a, b, (dims, ((), ())), preferred_element_type=F32)


def kernel(
    heads,
    groups,
    rand,
    gain_in,
    stream,
    cotangent,
    keys,
    values,
    stream_out,
    key_out,
    value_out,
    gain,
    hidden,
    upstream,
    queries,
    grad_query,
    handed,
    products,
    blocks,
    corner,
    halo,
    slot_keys,
    slot_values,
    terms,
    far_out,
    far_in,
    far_in2,
    mid_out,
    mid_in,
    near_out,
    near_in,
    edge_out,
    edge_in,
    global_out,
    global_in,
    line_sum,
    line_out,
    cross_in,
    cross_out,
    last_in,
    local_sem,
    kv_send,
    kv_recv,
    halo_send,
    halo_recv,
    corner_send,
    corner_recv,
    ret_send,
    ret_recv,
    edge_send,
    edge_recv,
    global_send,
    global_recv,
    cross_send,
    cross_recv,
    last_send,
    last_recv,
    handed_send,
    handed_recv,
):
    device = lax.axis_index("seq")
    section = lax.axis_index("section")
    sections = lax.axis_size("section")
    z, y = device // SIDE, device % SIDE
    wanted = rand[0, 0]
    pieces = 2 * groups
    per_group = heads // groups
    factor = HD ** (-0.5)
    edge = (y == 0) | (y == SIDE - 1)

    def at(direction, distance):
        if direction == 0:
            return z * SIDE + (y + distance) % SIDE
        if direction == 1:
            return z * SIDE + (y + SIDE - distance) % SIDE
        if direction == 2:
            return ((z + distance) % SIDE) * SIDE + y
        return ((z + SIDE - distance) % SIDE) * SIDE + y

    def remote(src, dst, send, recv, to):
        return pltpu.make_async_remote_copy(
            src_ref=src,
            dst_ref=dst,
            send_sem=send,
            recv_sem=recv,
            device_id={"seq": to},
            device_id_type=MESH,
        )

    def each(low, high, body):
        def step(i, carry):
            body(i)
            return carry

        lax.fori_loop(low, high, step, 0)

    own = []
    for g in range(groups):
        columns = pl.ds(g * HD, HD)
        own.append(pltpu.make_async_copy(keys.at[0, :, columns], blocks.at[0, 2 * g], local_sem.at[2 * g]))
        own.append(
            pltpu.make_async_copy(values.at[0, :, columns], blocks.at[0, 2 * g + 1], local_sem.at[2 * g + 1])
        )
    for copy in own:
        copy.start()
    load_gain = pltpu.make_async_copy(gain_in, gain, local_sem.at[pieces])
    load_hidden = pltpu.make_async_copy(stream.at[0], hidden, local_sem.at[pieces + 1])
    load_upstream = pltpu.make_async_copy(cotangent.at[0], upstream, local_sem.at[pieces + 2])
    load_gain.start()
    load_hidden.start()
    load_upstream.start()

    barrier = pltpu.get_barrier_semaphore()

    def greet(k):
        pl.semaphore_signal(barrier, inc=1, device_id={"seq": at(0, k)}, device_id_type=MESH)
        pl.semaphore_signal(barrier, inc=1, device_id={"seq": at(2, k)}, device_id_type=MESH)

    each(1, SIDE, greet)
    before = (section + sections - 1) % sections
    after = (section + 1) % sections
    pl.semaphore_signal(barrier, inc=1, device_id={"section": before}, device_id_type=MESH)
    pl.semaphore_signal(barrier, inc=1, device_id={"section": after}, device_id_type=MESH)
    for copy in own:
        copy.wait()
    pl.semaphore_wait(barrier, 2 * (SIDE - 1) + 2)

    line = (z, y)
    cross = (y, z)
    along = (2, 0)
    across = (0, 2)

    def corner_copy(stage, half, i, to, index):
        if stage == 0:
            src = blocks.at[0, 2 * (i // 2) + half, pl.ds((i % 2) * HALF, HALF)]
        else:
            src = corner.at[half, i]
        return remote(
            src, corner.at[half, i], corner_send.at[stage, half, index], corner_recv.at[half, i], to
        )

    @pl.when(device == 0)
    def _():
        corner[0, 0] = blocks[0, 0, :HALF]
        corner[1, 0] = blocks[0, 1, :HALF]

        def scatter(i):
            for half in range(2):
                corner_copy(0, half, i, at(along[half], i), i).start()

        each(1, SIDE, scatter)

    def slot(direction, step):
        return (step, SIDE - step, SIDE + step, 2 * SIDE - step)[direction]

    def kv(direction, step, g):
        part = pl.ds(2 * g, 2) if step <= 2 else pl.ds(2 * g + PAR[direction], 1)
        src = blocks.at[0 if step == 1 else slot(direction, step - 1), part]
        return remote(
            src,
            blocks.at[slot(direction, step), part],
            kv_send.at[direction, step - 1, g],
            kv_recv.at[direction, step - 1, g],
            at(direction, 1),
        )

    def halo_copy(g, source, to):
        part = pl.ds(2 * g, 2)
        return remote(blocks.at[source, part], halo.at[part], halo_send.at[g], halo_recv.at[g], to)

    def forward(step, g):
        for direction in range(DIRS):
            if step > 1:
                kv(direction, step - 1, g).wait_recv()
            kv(direction, step, g).start()
        if step == 2:

            @pl.when(y == SIDE - 1)
            def _():
                halo_copy(g, SIDE + 1, z * SIDE).start()

            @pl.when(y == 0)
            def _():
                halo_copy(g, 2 * SIDE - 1, z * SIDE + SIDE - 1).start()

    forward(1, 0)
    forward(1, 1)

    load_hidden.wait()

    def square(h, total):
        x = hidden[:, pl.ds(pl.multiple_of(h * HD, HD), HD)].astype(F32)
        return total + x * x

    squares = lax.fori_loop(0, heads, square, jnp.zeros((ROWS, HD), F32))
    inverse = lax.rsqrt(jnp.sum(squares, axis=1, keepdims=True) / (heads * HD) + 1e-05)
    load_gain.wait()

    def query(h):
        columns = pl.ds(pl.multiple_of(h * HD, HD), HD)
        normed = hidden[:, columns].astype(F32) * inverse
        queries[:, columns] = (normed * gain[:, columns]).astype(BF16)

    each(0, heads, query)
    products[...] = jnp.zeros_like(products)

    forward(2, 0)
    forward(1, 2)
    forward(2, 1)

    for half in range(2):

        @pl.when(cross[half] == 0)
        def _():
            @pl.when(line[half] != 0)
            def _():
                corner_copy(1, half, line[half], device, 0).wait_recv()

            def spread(k):
                corner_copy(1, half, line[half], at(across[half], k), k).start()

            each(1, SIDE, spread)

    forward(3, 0)
    forward(1, 3)
    forward(2, 2)
    forward(4, 0)
    forward(3, 1)

    for half in range(2):

        @pl.when(cross[half] != 0)
        def _():
            corner_copy(2, half, line[half], device, 0).wait_recv()

    def over_lines(k):
        for half in range(2):
            corner_copy(2, half, line[half], at(along[half], k), k).start()

    each(1, SIDE, over_lines)
    forward(2, 3)
    forward(3, 2)
    load_upstream.wait()

    def collect(g):
        for direction in range(DIRS):
            kv(direction, 4, g).wait_recv()

        @pl.when(edge)
        def _():
            halo_copy(g, 0, device).wait_recv()

        for half in range(2):
            for i in range(2):

                @pl.when(line[half] != 2 * g + i)
                def _():
                    corner_copy(2, half, 2 * g + i, device, 0).wait_recv()

    partners = (
        (y + 2 - 4 * ((y // 2) % 2), None),
        ((y + 4) % SIDE, None),
        (None, z + 1 - 2 * (z % 2)),
        (None, z + 2 - 4 * ((z // 2) % 2)),
        (None, (z + 4) % SIDE),
    )

    def assemble(g):
        for half, target in ((0, slot_keys), (1, slot_values)):
            piece = 2 * g + half
            target[g, pl.ds(0, ROWS)] = jnp.where(y == 0, halo[piece], blocks[1, piece])
            target[g, pl.ds(ROWS, ROWS)] = blocks[0, piece]
            target[g, pl.ds(2 * ROWS, ROWS)] = jnp.where(
                y == SIDE - 1, halo[piece], blocks[SIDE - 1, piece]
            )
            for i in range(2):
                target[g, pl.ds(3 * ROWS + i * HALF, HALF)] = corner[half, 2 * g + i]
            picked = None
            for to_y, to_z in partners:
                if to_z is None:
                    name, place = z * SIDE + to_y, (y + SIDE - to_y) % SIDE
                else:
                    name, place = to_z * SIDE + y, SIDE + (z + SIDE - to_z) % SIDE
                block = blocks[place, piece]
                picked = block if picked is None else jnp.where(wanted == name, block, picked)
            target[g, pl.ds(4 * ROWS, ROWS)] = picked

    no_before = jnp.where(device == 0, NEG, 0.0).astype(F32)
    no_after = jnp.where(device == SIDE * SIDE - 1, NEG, 0.0).astype(F32)
    bias = (no_before, None, no_after, no_before, None)
    scale = factor * math.log2(math.e)

    def unit(g, first_head, count, fresh):
        columns = [pl.ds(pl.multiple_of((first_head + i) * HD, HD), HD) for i in range(count)]
        q = jnp.concatenate([queries[:, c] for c in columns], axis=0)
        do = jnp.concatenate([upstream[:, c] for c in columns], axis=0)
        k, v = slot_keys[g], slot_values[g]
        raw = dot(k, q, ((1,), (1,)))
        grad_weights = dot(v, do, ((1,), (1,)))
        scores = []
        for i in range(5):
            part = raw[i * ROWS : (i + 1) * ROWS] * scale
            scores.append(part if bias[i] is None else part + bias[i])
        scores = jnp.concatenate(scores, axis=0)
        peak = jnp.max(scores, axis=0, keepdims=True)
        raised = jnp.exp2(scores - peak)
        weights = raised * (1.0 / jnp.sum(raised, axis=0, keepdims=True))
        row_dot = jnp.sum(weights * grad_weights, axis=0, keepdims=True)
        grad_low = (weights * (grad_weights - row_dot) * factor).astype(BF16)
        weights_low = weights.astype(BF16)
        key_terms = dot(grad_low, q, ((1,), (0,)))
        value_terms = dot(weights_low, do, ((1,), (0,)))
        if fresh:
            terms[2 * g] = key_terms
            terms[2 * g + 1] = value_terms
        else:
            terms[2 * g] += key_terms
            terms[2 * g + 1] += value_terms
        back = dot(grad_low, k, ((0,), (0,)))
        for i, c in enumerate(columns):
            grad_query[:, c] = back[i * ROWS : (i + 1) * ROWS]

    def mark(to):
        return jnp.where(wanted == to, 1.0, 0.0).astype(F32)

    before_rows, own_rows, after_rows, global_rows, random_rows = (
        pl.ds(i * ROWS, ROWS) for i in range(5)
    )

    def ret(direction, step, g):
        pair = {4: (far_out, far_in), 3: (far_in, far_in2), 2: (mid_out, mid_in), 1: (near_out, near_in)}
        src, dst = pair[step]
        return remote(
            src.at[direction, g],
            dst.at[direction, g],
            ret_send.at[direction, step - 1, g],
            ret_recv.at[direction, step - 1, g],
            at(direction, 1),
        )

    def global_copy(half, i, source, to):
        return remote(
            global_out.at[half, i],
            global_in.at[half, source],
            global_send.at[half, i],
            global_recv.at[half, source],
            to,
        )

    def edge_copy(g, to):
        part = pl.ds(2 * g, 2)
        return remote(edge_out.at[part], edge_in.at[part], edge_send.at[g], edge_recv.at[g], to)

    def cross_copy(src, dst, send, recv, half, source, to):
        return remote(src.at[half], dst.at[half, source], send.at[half], recv.at[half, source], to)

    def half_rows(i):
        return pl.ds(pl.multiple_of(3 * ROWS + (i % 2) * HALF, HALF), HALF)

    def send_far(g):
        for direction in range(DIRS):
            random = terms[2 * g + PAR[direction], random_rows]
            far_out[direction, g] = (random * mark(at(direction, 4))).astype(BF16)
            ret(direction, 4, g).start()
        for half in range(2):
            for j in range(2):
                i = 2 * g + j
                global_out[half, i] = terms[2 * g + half, pl.ds(3 * ROWS + j * HALF, HALF)].astype(BF16)

                @pl.when(line[half] != i)
                def _():
                    to = i * SIDE + y if half == 0 else z * SIDE + i
                    global_copy(half, i, line[half], to).start()

        @pl.when(y == SIDE - 1)
        def _():
            for half in range(2):
                edge_out[2 * g + half] = terms[2 * g + half, after_rows].astype(BF16)
            edge_copy(g, at(2, 1)).start()

        @pl.when(y == 0)
        def _():
            for half in range(2):
                edge_out[2 * g + half] = terms[2 * g + half, before_rows].astype(BF16)
            edge_copy(g, at(3, 1)).start()

    def pass_far(g):
        for direction in range(DIRS):
            ret(direction, 4, g).wait_recv()
            ret(direction, 3, g).start()

    def send_mid(g):
        for direction in range(DIRS):
            ret(direction, 3, g).wait_recv()
            here = mark(at(direction, 2))
            half = PAR[direction]
            mid_out[direction, g, half] = (
                terms[2 * g + half, random_rows] * here + far_in2[direction, g].astype(F32)
            ).astype(BF16)
            mid_out[direction, g, 1 - half] = (terms[2 * g + 1 - half, random_rows] * here).astype(BF16)
            ret(direction, 2, g).start()

    def send_near(g):
        @pl.when(edge)
        def _():
            edge_copy(g, device).wait_recv()

        for direction in range(DIRS):
            ret(direction, 2, g).wait_recv()
            for half in range(2):
                p = 2 * g + half
                passed = mid_in[direction, g, half].astype(F32)
                if direction == 0:
                    added = jnp.where(
                        y == SIDE - 1,
                        edge_in[p].astype(F32),
                        terms[p, after_rows].astype(BF16).astype(F32),
                    )
                elif direction == 1:
                    added = jnp.where(
                        y == 0,
                        edge_in[p].astype(F32),
                        terms[p, before_rows].astype(BF16).astype(F32),
                    )
                else:
                    added = terms[p, random_rows] * mark(at(direction, 1))
                near_out[direction, g, half] = (passed + added).astype(BF16)
            ret(direction, 1, g).start()

    def add_products(first_head, count):
        total = products[...]
        for i in range(count):
            columns = pl.ds(pl.multiple_of((first_head + i) * HD, HD), HD)
            normed = hidden[:, columns].astype(F32) * inverse
            total = total + grad_query[:, columns] * gain[:, columns] * normed
        products[...] = total

    half_group = per_group // 2

    def group_step(g):
        collect(g)
        assemble(g)
        unit(g, g * per_group, half_group, True)

        @pl.when(g == 0)
        def _():
            forward(4, 1)
            forward(3, 3)
            forward(4, 2)

        add_products(g * per_group, half_group)
        unit(g, g * per_group + half_group, half_group, False)

        @pl.when(g == 0)
        def _():
            forward(4, 3)

        send_far(g)

        @pl.when(g >= 1)
        def _():
            pass_far(g - 1)

        @pl.when(g >= 2)
        def _():
            send_mid(g - 2)

        @pl.when(g >= 3)
        def _():
            send_near(g - 3)

        add_products(g * per_group + half_group, half_group)

    each(0, groups, group_step)

    mean = jnp.sum(products[...], axis=1, keepdims=True) / (heads * HD)

    def hand_copy(part):
        columns = pl.ds(pl.multiple_of(part * (per_group * HD), per_group * HD), per_group * HD)
        return pltpu.make_async_remote_copy(
            src_ref=handed.at[:, columns],
            dst_ref=stream_out.at[0, :, columns],
            send_sem=handed_send.at[part],
            recv_sem=handed_recv.at[part],
            device_id={"section": before},
            device_id_type=MESH,
        )

    def hand(part):
        for i in range(per_group):
            columns = pl.ds(pl.multiple_of((part * per_group + i) * HD, HD), HD)
            normed = hidden[:, columns].astype(F32) * inverse
            grad_norm = grad_query[:, columns] * gain[:, columns]
            grad = inverse * (grad_norm - normed * mean)
            handed[:, columns] = (upstream[:, columns].astype(F32) + grad).astype(BF16)
        hand_copy(part).start()

    each(0, groups, hand)

    for g in range(1, groups):
        if g == 1:
            pass_far(3)
        if g <= 2:
            send_mid(g + 1)
        send_near(g)
        if g == 1:
            for half in range(2):
                start = terms[2 * (line[half] // 2) + half, half_rows(line[half])]

                def add_line(k, total):
                    source = (line[half] + k) % SIDE
                    global_copy(half, 0, source, device).wait_recv()
                    return total + global_in[half, source].astype(F32)

                line_sum[half] = lax.fori_loop(1, SIDE, add_line, start)

                @pl.when(cross[half] != 0)
                def _():
                    line_out[half] = line_sum[half].astype(BF16)
                    to = z * SIDE if half == 0 else y
                    cross_copy(line_out, cross_in, cross_send, cross_recv, half, cross[half], to).start()

        if g == 2:
            for half in range(2):

                @pl.when(cross[half] == 0)
                def _():
                    def add_cross(k, total):
                        cross_copy(line_out, cross_in, cross_send, cross_recv, half, k, device).wait_recv()
                        return total + cross_in[half, k].astype(F32)

                    line_sum[half] = lax.fori_loop(1, SIDE, add_cross, line_sum[half])

                    @pl.when(line[half] != 0)
                    def _():
                        cross_out[half] = line_sum[half].astype(BF16)
                        cross_copy(cross_out, last_in, last_send, last_recv, half, line[half], 0).start()

    @pl.when(device == 0)
    def _():
        for half in range(2):

            def take(i):
                cross_copy(cross_out, last_in, last_send, last_recv, half, i, device).wait_recv()
                rows = pl.ds(pl.multiple_of(ROWS + (i % 2) * HALF, HALF), HALF)
                terms[2 * (i // 2) + half, rows] += last_in[half, i].astype(F32)

            each(1, SIDE, take)
            terms[half, pl.ds(ROWS, HALF)] += line_sum[half]

    for g in range(groups):
        for direction in range(DIRS):
            ret(direction, 1, g).wait_recv()
        for half, out in ((0, key_out), (1, value_out)):
            total = terms[2 * g + half, own_rows]
            for direction in range(DIRS):
                total = total + near_in[direction, g, half].astype(F32)
            out[0, :, pl.ds(g * HD, HD)] = total.astype(BF16)

    def sent(g):
        for direction in range(DIRS):
            for step in (1, 2, 3, 4):
                kv(direction, step, g).wait_send()
                ret(direction, step, g).wait_send()

        @pl.when(edge)
        def _():
            halo_copy(g, 0, device).wait_send()
            edge_copy(g, device).wait_send()

    each(0, groups, sent)

    for half in range(2):

        def sent_pieces(k):
            corner_copy(2, half, 0, device, k).wait_send()
            global_copy(half, (line[half] + k) % SIDE, 0, device).wait_send()

        each(1, SIDE, sent_pieces)

        @pl.when(cross[half] == 0)
        def _():
            def sent_across(k):
                corner_copy(1, half, 0, device, k).wait_send()

            each(1, SIDE, sent_across)

            @pl.when(line[half] != 0)
            def _():
                cross_copy(cross_out, last_in, last_send, last_recv, half, 0, device).wait_send()

        @pl.when(cross[half] != 0)
        def _():
            cross_copy(line_out, cross_in, cross_send, cross_recv, half, 0, device).wait_send()

    @pl.when(device == 0)
    def _():
        def sent_corner(i):
            for half in range(2):
                corner_copy(0, half, i, device, i).wait_send()

        each(1, SIDE, sent_corner)

    for part in range(groups):
        hand_copy(part).wait()


def solution(mesh):
    def on_device(stream, cotangent, keys, values, gain, rand_blocks):
        heads = stream.shape[2] // HD
        groups = keys.shape[2] // HD
        pieces = 2 * groups
        block = (ROWS, HD)
        part = (HALF, HD)
        vmem = pl.BlockSpec(memory_space=pltpu.VMEM)
        hbm = pl.BlockSpec(memory_space=pl.ANY)
        dma = pltpu.SemaphoreType.DMA

        def bf16(*shape):
            return pltpu.VMEM(shape, BF16)

        def f32(*shape):
            return pltpu.VMEM(shape, F32)

        def body(*refs):
            kernel(heads, groups, *refs)

        return pl.pallas_call(
            body,
            name="relay",
            out_shape=(
                jax.ShapeDtypeStruct(stream.shape, BF16),
                jax.ShapeDtypeStruct(keys.shape, BF16),
                jax.ShapeDtypeStruct(values.shape, BF16),
            ),
            in_specs=[pl.BlockSpec(memory_space=pltpu.SMEM), hbm, hbm, hbm, hbm, hbm],
            out_specs=(hbm, vmem, vmem),
            scratch_shapes=[
                f32(1, heads * HD),
                bf16(ROWS, heads * HD),
                bf16(ROWS, heads * HD),
                bf16(ROWS, heads * HD),
                f32(ROWS, heads * HD),
                bf16(ROWS, heads * HD),
                f32(*block),
                bf16(2 * SIDE, pieces, *block),
                bf16(2, SIDE, *part),
                bf16(pieces, *block),
                bf16(groups, 5 * ROWS, HD),
                bf16(groups, 5 * ROWS, HD),
                f32(pieces, 5 * ROWS, HD),
                bf16(DIRS, groups, *block),
                bf16(DIRS, groups, *block),
                bf16(DIRS, groups, *block),
                bf16(DIRS, groups, 2, *block),
                bf16(DIRS, groups, 2, *block),
                bf16(DIRS, groups, 2, *block),
                bf16(DIRS, groups, 2, *block),
                bf16(pieces, *block),
                bf16(pieces, *block),
                bf16(2, SIDE, *part),
                bf16(2, SIDE, *part),
                f32(2, *part),
                bf16(2, *part),
                bf16(2, SIDE, *part),
                bf16(2, *part),
                bf16(2, SIDE, *part),
                dma((pieces + 3,)),
                dma((DIRS, 4, groups)),
                dma((DIRS, 4, groups)),
                dma((groups,)),
                dma((groups,)),
                dma((3, 2, SIDE)),
                dma((2, SIDE)),
                dma((DIRS, 4, groups)),
                dma((DIRS, 4, groups)),
                dma((groups,)),
                dma((groups,)),
                dma((2, SIDE)),
                dma((2, SIDE)),
                dma((2,)),
                dma((2, SIDE)),
                dma((2,)),
                dma((2, SIDE)),
                dma((groups,)),
                dma((groups,)),
            ],
            compiler_params=pltpu.CompilerParams(
                collective_id=0, has_side_effects=True, vmem_limit_bytes=60 * 1024 * 1024
            ),
        )(rand_blocks, gain, stream, cotangent, keys, values)

    return jax.shard_map(
        on_device,
        mesh=mesh,
        in_specs=(
            P("section", "seq", None),
            P("section", "seq", None),
            P("section", "seq", None),
            P("section", "seq", None),
            P("section", None),
            P("seq", None),
        ),
        out_specs=(P("section", "seq", None), P("section", "seq", None), P("section", "seq", None)),
        check_vma=False,
    )
```

```python
import math

import jax
import jax.numpy as jnp
from jax import lax
from jax.experimental import pallas as pl
from jax.experimental.pallas import tpu as pltpu
from jax.sharding import PartitionSpec as P

MESH = pl.DeviceIdType.MESH
HD = 128
ROWS = 128
HALF = ROWS // 2
SQUARE = 4
NEG = -1e30
F32 = jnp.float32
BF16 = jnp.bfloat16
VMEM_LIMIT = 48 * 1024 * 1024
SIDE = 8
DIRS = 4
PAR = (0, 1, 0, 1)


def dot(a, b, dims):
    return lax.dot_general(a, b, (dims, ((), ())), preferred_element_type=F32)


def kernel(
    heads,
    groups,
    rand,
    gain_in,
    stream,
    cotangent,
    keys,
    values,
    stream_out,
    key_out,
    value_out,
    gain,
    hidden,
    upstream,
    queries,
    grad_query,
    handed,
    arrived,
    hidden_after,
    mean_out,
    mean_in,
    products,
    blocks,
    corner,
    halo,
    slot_keys,
    slot_values,
    terms,
    far_out,
    far_in,
    far_in2,
    mid_out,
    mid_in,
    near_out,
    near_in,
    edge_out,
    edge_in,
    global_out,
    global_in,
    line_sum,
    line_out,
    cross_in,
    cross_out,
    last_in,
    local_sem,
    kv_send,
    kv_recv,
    halo_send,
    halo_recv,
    corner_send,
    corner_recv,
    ret_send,
    ret_recv,
    edge_send,
    edge_recv,
    global_send,
    global_recv,
    cross_send,
    cross_recv,
    last_send,
    last_recv,
    handed_send,
    handed_recv,
    hidden_sem,
    mean_sem,
):
    device = lax.axis_index("seq")
    section = lax.axis_index("section")
    sections = lax.axis_size("section")
    z, y = device // SIDE, device % SIDE
    wanted = rand[0, 0]
    pieces = 2 * groups
    per_group = heads // groups
    factor = HD ** (-0.5)
    edge = (y == 0) | (y == SIDE - 1)

    def at(direction, distance):
        if direction == 0:
            return z * SIDE + (y + distance) % SIDE
        if direction == 1:
            return z * SIDE + (y + SIDE - distance) % SIDE
        if direction == 2:
            return ((z + distance) % SIDE) * SIDE + y
        return ((z + SIDE - distance) % SIDE) * SIDE + y

    def remote(src, dst, send, recv, to):
        return pltpu.make_async_remote_copy(
            src_ref=src,
            dst_ref=dst,
            send_sem=send,
            recv_sem=recv,
            device_id={"seq": to},
            device_id_type=MESH,
        )

    def each(low, high, body):
        def step(i, carry):
            body(i)
            return carry

        lax.fori_loop(low, high, step, 0)

    own = []
    for g in range(groups):
        columns = pl.ds(g * HD, HD)
        own.append(pltpu.make_async_copy(keys.at[0, :, columns], blocks.at[0, 2 * g], local_sem.at[2 * g]))
        own.append(
            pltpu.make_async_copy(values.at[0, :, columns], blocks.at[0, 2 * g + 1], local_sem.at[2 * g + 1])
        )
    for copy in own:
        copy.start()
    load_gain = pltpu.make_async_copy(gain_in, gain, local_sem.at[pieces])
    load_hidden = pltpu.make_async_copy(stream.at[0], hidden, local_sem.at[pieces + 1])
    load_upstream = pltpu.make_async_copy(cotangent.at[0], upstream, local_sem.at[pieces + 2])
    load_gain.start()
    load_hidden.start()
    load_upstream.start()

    barrier = pltpu.get_barrier_semaphore()

    def greet(k):
        pl.semaphore_signal(barrier, inc=1, device_id={"seq": at(0, k)}, device_id_type=MESH)
        pl.semaphore_signal(barrier, inc=1, device_id={"seq": at(2, k)}, device_id_type=MESH)

    each(1, SIDE, greet)
    before = (section + sections - 1) % sections
    after = (section + 1) % sections
    pl.semaphore_signal(barrier, inc=1, device_id={"section": before}, device_id_type=MESH)
    pl.semaphore_signal(barrier, inc=1, device_id={"section": after}, device_id_type=MESH)
    for copy in own:
        copy.wait()
    pl.semaphore_wait(barrier, 2 * (SIDE - 1) + 2)

    line = (z, y)
    cross = (y, z)
    along = (2, 0)
    across = (0, 2)

    def corner_copy(stage, half, i, to, index):
        if stage == 0:
            src = blocks.at[0, 2 * (i // 2) + half, pl.ds((i % 2) * HALF, HALF)]
        else:
            src = corner.at[half, i]
        return remote(
            src, corner.at[half, i], corner_send.at[stage, half, index], corner_recv.at[half, i], to
        )

    @pl.when(device == 0)
    def _():
        corner[0, 0] = blocks[0, 0, :HALF]
        corner[1, 0] = blocks[0, 1, :HALF]

        def scatter(i):
            for half in range(2):
                corner_copy(0, half, i, at(along[half], i), i).start()

        each(1, SIDE, scatter)

    def slot(direction, step):
        return (step, SIDE - step, SIDE + step, 2 * SIDE - step)[direction]

    def both_halves(condition, direction, step, g, act):
        if condition is None:
            act(direction, step, g, step <= 2)
            return

        @pl.when(condition)
        def _():
            act(direction, step, g, True)

        @pl.when(jnp.logical_not(condition))
        def _():
            act(direction, step, g, False)

    def middle(i):
        return (i % SQUARE == 1) | (i % SQUARE == 2)

    def kv_whole(direction, step, sender):
        if step > 2:
            return None
        if step == 2:
            if sender:
                return middle(y if direction < 2 else z)
            return middle((y + SIDE - 1, y + 1, z + SIDE - 1, z + 1)[direction])
        if direction == 0:
            return y != (SIDE - 1 if sender else 0)
        if direction == 1:
            return y != (0 if sender else SIDE - 1)
        if direction == 2:
            return (z % SQUARE != (3 if sender else 0)) | (y == SIDE - 1)
        return (z % SQUARE != (0 if sender else 3)) | (y == 0)

    def kv(direction, step, g, whole):
        part = pl.ds(2 * g, 2) if whole else pl.ds(2 * g + PAR[direction], 1)
        src = blocks.at[0 if step == 1 else slot(direction, step - 1), part]
        return remote(
            src,
            blocks.at[slot(direction, step), part],
            kv_send.at[direction, step - 1, g],
            kv_recv.at[direction, step - 1, g],
            at(direction, 1),
        )

    def kv_start(*what):
        kv(*what).start()

    def kv_arrived(*what):
        kv(*what).wait_recv()

    def kv_left(*what):
        kv(*what).wait_send()

    def halo_copy(g, source, to):
        part = pl.ds(2 * g, 2)
        return remote(blocks.at[source, part], halo.at[part], halo_send.at[g], halo_recv.at[g], to)

    def forward(step, g):
        for direction in range(DIRS):
            if step > 1:
                both_halves(kv_whole(direction, step - 1, False), direction, step - 1, g, kv_arrived)
            both_halves(kv_whole(direction, step, True), direction, step, g, kv_start)
        if step == 2:

            @pl.when(y == SIDE - 1)
            def _():
                halo_copy(g, SIDE + 1, z * SIDE).start()

            @pl.when(y == 0)
            def _():
                halo_copy(g, 2 * SIDE - 1, z * SIDE + SIDE - 1).start()

    forward(1, 0)
    forward(1, 1)
    forward(1, 2)

    hidden_copy = pltpu.make_async_remote_copy(
        src_ref=stream.at[0],
        dst_ref=hidden_after,
        send_sem=hidden_sem.at[0],
        recv_sem=hidden_sem.at[1],
        device_id={"section": before},
        device_id_type=MESH,
    )
    hidden_copy.start()

    load_hidden.wait()

    def square(h, total):
        x = hidden[:, pl.ds(pl.multiple_of(h * HD, HD), HD)].astype(F32)
        return total + x * x

    squares = lax.fori_loop(0, heads, square, jnp.zeros((ROWS, HD), F32))
    inverse = lax.rsqrt(jnp.sum(squares, axis=1, keepdims=True) / (heads * HD) + 1e-05)
    load_gain.wait()

    def query(h):
        columns = pl.ds(pl.multiple_of(h * HD, HD), HD)
        normed = hidden[:, columns].astype(F32) * inverse
        queries[:, columns] = (normed * gain[:, columns]).astype(BF16)

    each(0, heads, query)
    products[...] = jnp.zeros_like(products)

    forward(2, 0)
    forward(2, 1)
    forward(1, 3)

    for half in range(2):

        @pl.when(cross[half] == 0)
        def _():
            @pl.when(line[half] != 0)
            def _():
                corner_copy(1, half, line[half], device, 0).wait_recv()

            def spread(k):
                corner_copy(1, half, line[half], at(across[half], k), k).start()

            each(1, SIDE, spread)

    forward(3, 0)
    forward(2, 2)
    forward(3, 1)
    forward(4, 0)

    for half in range(2):

        @pl.when(cross[half] != 0)
        def _():
            corner_copy(2, half, line[half], device, 0).wait_recv()

    def over_lines(k):
        for half in range(2):
            corner_copy(2, half, line[half], at(along[half], k), k).start()

    each(1, SIDE, over_lines)
    forward(2, 3)
    forward(3, 2)
    load_upstream.wait()

    def collect(g):
        for direction in range(DIRS):
            kv(direction, 4, g, False).wait_recv()

        @pl.when(edge)
        def _():
            halo_copy(g, 0, device).wait_recv()

        for half in range(2):
            for i in range(2):

                @pl.when(line[half] != 2 * g + i)
                def _():
                    corner_copy(2, half, 2 * g + i, device, 0).wait_recv()

    partners = (
        (y + 2 - 4 * ((y // 2) % 2), None),
        ((y + 4) % SIDE, None),
        (None, z + 1 - 2 * (z % 2)),
        (None, z + 2 - 4 * ((z // 2) % 2)),
        (None, (z + 4) % SIDE),
    )

    def assemble(g):
        for half, target in ((0, slot_keys), (1, slot_values)):
            piece = 2 * g + half
            target[g, pl.ds(0, ROWS)] = jnp.where(y == 0, halo[piece], blocks[1, piece])
            target[g, pl.ds(ROWS, ROWS)] = blocks[0, piece]
            target[g, pl.ds(2 * ROWS, ROWS)] = jnp.where(
                y == SIDE - 1, halo[piece], blocks[SIDE - 1, piece]
            )
            for i in range(2):
                target[g, pl.ds(3 * ROWS + i * HALF, HALF)] = corner[half, 2 * g + i]
            picked = None
            for to_y, to_z in partners:
                if to_z is None:
                    name, place = z * SIDE + to_y, (y + SIDE - to_y) % SIDE
                else:
                    name, place = to_z * SIDE + y, SIDE + (z + SIDE - to_z) % SIDE
                block = blocks[place, piece]
                picked = block if picked is None else jnp.where(wanted == name, block, picked)
            target[g, pl.ds(4 * ROWS, ROWS)] = picked

    no_before = jnp.where(device == 0, NEG, 0.0).astype(F32)
    no_after = jnp.where(device == SIDE * SIDE - 1, NEG, 0.0).astype(F32)
    bias = (no_before, None, no_after, no_before, None)
    scale = factor * math.log2(math.e)

    def unit(g, first_head, count, fresh):
        columns = [pl.ds(pl.multiple_of((first_head + i) * HD, HD), HD) for i in range(count)]
        q = jnp.concatenate([queries[:, c] for c in columns], axis=0)
        do = jnp.concatenate([upstream[:, c] for c in columns], axis=0)
        k, v = slot_keys[g], slot_values[g]
        raw = dot(k, q, ((1,), (1,)))
        grad_weights = dot(v, do, ((1,), (1,)))
        scores = []
        for i in range(5):
            part = raw[i * ROWS : (i + 1) * ROWS] * scale
            scores.append(part if bias[i] is None else part + bias[i])
        scores = jnp.concatenate(scores, axis=0)
        peak = jnp.max(scores, axis=0, keepdims=True)
        raised = jnp.exp2(scores - peak)
        weights = raised * (1.0 / jnp.sum(raised, axis=0, keepdims=True))
        row_dot = jnp.sum(weights * grad_weights, axis=0, keepdims=True)
        grad_low = (weights * (grad_weights - row_dot) * factor).astype(BF16)
        weights_low = weights.astype(BF16)
        key_terms = dot(grad_low, q, ((1,), (0,)))
        value_terms = dot(weights_low, do, ((1,), (0,)))
        if fresh:
            terms[2 * g] = key_terms
            terms[2 * g + 1] = value_terms
        else:
            terms[2 * g] += key_terms
            terms[2 * g + 1] += value_terms
        back = dot(grad_low, k, ((0,), (0,)))
        for i, c in enumerate(columns):
            grad_query[:, c] = back[i * ROWS : (i + 1) * ROWS]

    def mark(to):
        return jnp.where(wanted == to, 1.0, 0.0).astype(F32)

    before_rows, own_rows, after_rows, global_rows, random_rows = (
        pl.ds(i * ROWS, ROWS) for i in range(5)
    )

    def ret_whole(direction, step, sender):
        if step > 2:
            return None
        if step == 2:
            i = y if direction < 2 else z
            if not sender:
                i = i + (SIDE - 1, 1, SIDE - 1, 1)[direction]
            low = (i % SQUARE) < 2
            return low if direction in (0, 2) else jnp.logical_not(low)
        if direction == 0:
            return y != (SIDE - 1 if sender else 0)
        if direction == 1:
            return y != (0 if sender else SIDE - 1)
        if direction == 2:
            return (z % SQUARE != (3 if sender else 0)) | (y == 0)
        return (z % SQUARE != (0 if sender else 3)) | (y == SIDE - 1)

    def ret(direction, step, g, whole):
        pair = {4: (far_out, far_in), 3: (far_in, far_in2), 2: (mid_out, mid_in), 1: (near_out, near_in)}
        src, dst = pair[step]
        if step > 2:
            src, dst = src.at[direction, g], dst.at[direction, g]
        else:
            part = pl.ds(0, 2) if whole else pl.ds(PAR[direction], 1)
            src, dst = src.at[direction, g, part], dst.at[direction, g, part]
        return remote(
            src,
            dst,
            ret_send.at[direction, step - 1, g],
            ret_recv.at[direction, step - 1, g],
            at(direction, 1),
        )

    def ret_start(direction, step, g):
        def start(*what):
            ret(*what).start()

        both_halves(ret_whole(direction, step, True), direction, step, g, start)

    def ret_arrived(direction, step, g):
        def wait(*what):
            ret(*what).wait_recv()

        both_halves(ret_whole(direction, step, False), direction, step, g, wait)

    def ret_left(*what):
        ret(*what).wait_send()

    def received(buffer, direction, step, g, half):
        value = buffer[direction, g, half].astype(F32)
        if half == PAR[direction]:
            return value
        return jnp.where(ret_whole(direction, step, False), value, 0.0)

    def global_copy(half, i, source, to):
        return remote(
            global_out.at[half, i],
            global_in.at[half, source],
            global_send.at[half, i],
            global_recv.at[half, source],
            to,
        )

    def edge_copy(g, to):
        part = pl.ds(2 * g, 2)
        return remote(edge_out.at[part], edge_in.at[part], edge_send.at[g], edge_recv.at[g], to)

    def cross_copy(src, dst, send, recv, half, source, to):
        return remote(src.at[half], dst.at[half, source], send.at[half], recv.at[half, source], to)

    def half_rows(i):
        return pl.ds(pl.multiple_of(3 * ROWS + (i % 2) * HALF, HALF), HALF)

    def send_far(g):
        for direction in range(DIRS):
            random = terms[2 * g + PAR[direction], random_rows]
            far_out[direction, g] = (random * mark(at(direction, 4))).astype(BF16)
            ret_start(direction, 4, g)
        for half in range(2):
            for j in range(2):
                i = 2 * g + j
                global_out[half, i] = terms[2 * g + half, pl.ds(3 * ROWS + j * HALF, HALF)].astype(BF16)

                @pl.when(line[half] != i)
                def _():
                    to = i * SIDE + y if half == 0 else z * SIDE + i
                    global_copy(half, i, line[half], to).start()

        @pl.when(y == SIDE - 1)
        def _():
            for half in range(2):
                edge_out[2 * g + half] = terms[2 * g + half, after_rows].astype(BF16)
            edge_copy(g, z * SIDE).start()

        @pl.when(y == 0)
        def _():
            for half in range(2):
                edge_out[2 * g + half] = terms[2 * g + half, before_rows].astype(BF16)
            edge_copy(g, z * SIDE + SIDE - 1).start()

    def pass_far(g):
        for direction in range(DIRS):
            ret_arrived(direction, 4, g)
            ret_start(direction, 3, g)

    def send_mid(g):
        for direction in range(DIRS):
            ret_arrived(direction, 3, g)
            here = mark(at(direction, 2))
            half = PAR[direction]
            mid_out[direction, g, half] = (
                terms[2 * g + half, random_rows] * here + far_in2[direction, g].astype(F32)
            ).astype(BF16)
            mid_out[direction, g, 1 - half] = (terms[2 * g + 1 - half, random_rows] * here).astype(BF16)
            ret_start(direction, 2, g)

    def send_near(g):
        @pl.when(edge)
        def _():
            edge_copy(g, device).wait_recv()

        for direction in range(DIRS):
            ret_arrived(direction, 2, g)
            for half in range(2):
                p = 2 * g + half
                passed = received(mid_in, direction, 2, g, half)
                if direction < 2:
                    rows = after_rows if direction == 0 else before_rows
                    added = jnp.where(
                        y == (SIDE - 1 if direction == 0 else 0),
                        0.0,
                        terms[p, rows].astype(BF16).astype(F32),
                    )
                else:
                    added = terms[p, random_rows] * mark(at(direction, 1)) + jnp.where(
                        y == (0 if direction == 2 else SIDE - 1), edge_in[p].astype(F32), 0.0
                    )
                near_out[direction, g, half] = (passed + added).astype(BF16)
            ret_start(direction, 1, g)

    def to_before(src, dst, send, recv):
        return pltpu.make_async_remote_copy(
            src_ref=src,
            dst_ref=dst,
            send_sem=send,
            recv_sem=recv,
            device_id={"section": before},
            device_id_type=MESH,
        )

    def hand_copy(part):
        columns = pl.ds(pl.multiple_of(part * (per_group * HD), per_group * HD), per_group * HD)
        return to_before(
            handed.at[:, columns], arrived.at[:, columns], handed_send.at[part], handed_recv.at[part]
        )

    def mean_copy():
        return to_before(mean_out, mean_in, mean_sem.at[0], mean_sem.at[1])

    def hand(first_head, count):
        total = products[...]
        for i in range(count):
            columns = pl.ds(pl.multiple_of((first_head + i) * HD, HD), HD)
            grad_norm = grad_query[:, columns] * gain[:, columns]
            total = total + grad_norm * (hidden[:, columns].astype(F32) * inverse)
            handed[:, columns] = (upstream[:, columns].astype(F32) + inverse * grad_norm).astype(BF16)
        products[...] = total

    half_group = per_group // 2

    def group_step(g):
        collect(g)
        assemble(g)
        unit(g, g * per_group, half_group, True)


        @pl.when(g == 0)
        def _():
            forward(4, 1)
            forward(3, 3)
            forward(4, 2)

        hand(g * per_group, half_group)
        unit(g, g * per_group + half_group, half_group, False)

        send_far(g)

        @pl.when(g == 0)
        def _():
            forward(4, 3)

        hand(g * per_group + half_group, half_group)
        hand_copy(g).start()

        @pl.when(g >= 1)
        def _():
            pass_far(g - 1)

        @pl.when(g >= 2)
        def _():
            send_mid(g - 2)

        @pl.when(g >= 3)
        def _():
            send_near(g - 3)

    each(0, groups, group_step)

    mean = jnp.sum(products[...], axis=1, keepdims=True) / (heads * HD)
    mean_out[...] = jnp.broadcast_to(inverse * inverse * mean, (ROWS, HD))
    mean_copy().start()

    def receive_hand():
        hidden_copy.wait_recv()
        mean_copy().wait_recv()
        for part in range(groups):
            hand_copy(part).wait_recv()

        def finish(h):
            columns = pl.ds(pl.multiple_of(h * HD, HD), HD)
            along_input = hidden_after[:, columns].astype(F32) * mean_in[...]
            stream_out[0, :, columns] = (arrived[:, columns].astype(F32) - along_input).astype(BF16)

        each(0, heads, finish)

    for g in range(1, groups):
        if g == 1:
            pass_far(3)
        if g <= 2:
            send_mid(g + 1)
        if g == 3:
            receive_hand()
        send_near(g)
        if g == 1:
            for half in range(2):
                start = terms[2 * (line[half] // 2) + half, half_rows(line[half])]

                def add_line(k, total):
                    source = (line[half] + k) % SIDE
                    global_copy(half, 0, source, device).wait_recv()
                    return total + global_in[half, source].astype(F32)

                line_sum[half] = lax.fori_loop(1, SIDE, add_line, start)

                @pl.when(cross[half] != 0)
                def _():
                    line_out[half] = line_sum[half].astype(BF16)
                    to = z * SIDE if half == 0 else y
                    cross_copy(line_out, cross_in, cross_send, cross_recv, half, cross[half], to).start()

        if g == 2:
            for half in range(2):

                @pl.when(cross[half] == 0)
                def _():
                    def add_cross(k, total):
                        cross_copy(line_out, cross_in, cross_send, cross_recv, half, k, device).wait_recv()
                        return total + cross_in[half, k].astype(F32)

                    line_sum[half] = lax.fori_loop(1, SIDE, add_cross, line_sum[half])

                    @pl.when(line[half] != 0)
                    def _():
                        cross_out[half] = line_sum[half].astype(BF16)
                        cross_copy(cross_out, last_in, last_send, last_recv, half, line[half], 0).start()

    @pl.when(device == 0)
    def _():
        for half in range(2):

            def take(i):
                cross_copy(cross_out, last_in, last_send, last_recv, half, i, device).wait_recv()
                rows = pl.ds(pl.multiple_of(ROWS + (i % 2) * HALF, HALF), HALF)
                terms[2 * (i // 2) + half, rows] += last_in[half, i].astype(F32)

            each(1, SIDE, take)
            terms[half, pl.ds(ROWS, HALF)] += line_sum[half]

    for g in range(groups):
        for direction in range(DIRS):
            ret_arrived(direction, 1, g)
        for half, out in ((0, key_out), (1, value_out)):
            total = terms[2 * g + half, own_rows]
            for direction in range(DIRS):
                total = total + received(near_in, direction, 1, g, half)
            out[0, :, pl.ds(g * HD, HD)] = total.astype(BF16)

    def sent(g):
        for direction in range(DIRS):
            for step in (1, 2, 3, 4):
                both_halves(kv_whole(direction, step, True), direction, step, g, kv_left)
                both_halves(ret_whole(direction, step, True), direction, step, g, ret_left)

        @pl.when(edge)
        def _():
            halo_copy(g, 0, device).wait_send()
            edge_copy(g, device).wait_send()

    each(0, groups, sent)

    for half in range(2):

        def sent_pieces(k):
            corner_copy(2, half, 0, device, k).wait_send()
            global_copy(half, (line[half] + k) % SIDE, 0, device).wait_send()

        each(1, SIDE, sent_pieces)

        @pl.when(cross[half] == 0)
        def _():
            def sent_across(k):
                corner_copy(1, half, 0, device, k).wait_send()

            each(1, SIDE, sent_across)

            @pl.when(line[half] != 0)
            def _():
                cross_copy(cross_out, last_in, last_send, last_recv, half, 0, device).wait_send()

        @pl.when(cross[half] != 0)
        def _():
            cross_copy(line_out, cross_in, cross_send, cross_recv, half, 0, device).wait_send()

    @pl.when(device == 0)
    def _():
        def sent_corner(i):
            for half in range(2):
                corner_copy(0, half, i, device, i).wait_send()

        each(1, SIDE, sent_corner)

    hidden_copy.wait_send()
    mean_copy().wait_send()
    for part in range(groups):
        hand_copy(part).wait_send()


def solution(mesh):
    def on_device(stream, cotangent, keys, values, gain, rand_blocks):
        heads = stream.shape[2] // HD
        groups = keys.shape[2] // HD
        pieces = 2 * groups
        block = (ROWS, HD)
        part = (HALF, HD)
        vmem = pl.BlockSpec(memory_space=pltpu.VMEM)
        hbm = pl.BlockSpec(memory_space=pltpu.HBM)
        dma = pltpu.SemaphoreType.DMA

        def bf16(*shape):
            return pltpu.VMEM(shape, BF16)

        def f32(*shape):
            return pltpu.VMEM(shape, F32)

        def in_hbm(array):
            return pltpu.with_memory_space_constraint(array, pltpu.HBM)

        def body(*refs):
            kernel(heads, groups, *refs)

        results = pl.pallas_call(
            body,
            name="relay",
            out_shape=(
                jax.ShapeDtypeStruct(stream.shape, BF16),
                jax.ShapeDtypeStruct(keys.shape, BF16),
                jax.ShapeDtypeStruct(values.shape, BF16),
            ),
            in_specs=[pl.BlockSpec(memory_space=pltpu.SMEM), hbm, hbm, hbm, hbm, hbm],
            out_specs=(vmem, vmem, vmem),
            scratch_shapes=[
                f32(1, heads * HD),
                bf16(ROWS, heads * HD),
                bf16(ROWS, heads * HD),
                bf16(ROWS, heads * HD),
                f32(ROWS, heads * HD),
                bf16(ROWS, heads * HD),
                bf16(ROWS, heads * HD),
                bf16(ROWS, heads * HD),
                f32(*block),
                f32(*block),
                f32(*block),
                bf16(2 * SIDE, pieces, *block),
                bf16(2, SIDE, *part),
                bf16(pieces, *block),
                bf16(groups, 5 * ROWS, HD),
                bf16(groups, 5 * ROWS, HD),
                f32(pieces, 5 * ROWS, HD),
                bf16(DIRS, groups, *block),
                bf16(DIRS, groups, *block),
                bf16(DIRS, groups, *block),
                bf16(DIRS, groups, 2, *block),
                bf16(DIRS, groups, 2, *block),
                bf16(DIRS, groups, 2, *block),
                bf16(DIRS, groups, 2, *block),
                bf16(pieces, *block),
                bf16(pieces, *block),
                bf16(2, SIDE, *part),
                bf16(2, SIDE, *part),
                f32(2, *part),
                bf16(2, *part),
                bf16(2, SIDE, *part),
                bf16(2, *part),
                bf16(2, SIDE, *part),
                dma((pieces + 3,)),
                dma((DIRS, 4, groups)),
                dma((DIRS, 4, groups)),
                dma((groups,)),
                dma((groups,)),
                dma((3, 2, SIDE)),
                dma((2, SIDE)),
                dma((DIRS, 4, groups)),
                dma((DIRS, 4, groups)),
                dma((groups,)),
                dma((groups,)),
                dma((2, SIDE)),
                dma((2, SIDE)),
                dma((2,)),
                dma((2, SIDE)),
                dma((2,)),
                dma((2, SIDE)),
                dma((groups,)),
                dma((groups,)),
                dma((2,)),
                dma((2,)),
            ],
            compiler_params=pltpu.CompilerParams(
                collective_id=0, has_side_effects=True, vmem_limit_bytes=VMEM_LIMIT
            ),
        )(rand_blocks, *(in_hbm(a) for a in (gain, stream, cotangent, keys, values)))

        def write(*refs):
            sources, targets, sems = refs[:3], refs[3:6], refs[6]
            copies = [
                pltpu.make_async_copy(src, dst, sems.at[i])
                for i, (src, dst) in enumerate(zip(sources, targets))
            ]
            for copy in copies:
                copy.start()
            for copy in copies:
                copy.wait()

        return pl.pallas_call(
            write,
            name="write",
            out_shape=tuple(jax.ShapeDtypeStruct(r.shape, r.dtype) for r in results),
            in_specs=[pl.BlockSpec(memory_space=pl.ANY)] * 3,
            out_specs=(hbm,) * 3,
            scratch_shapes=[dma((3,))],
            compiler_params=pltpu.CompilerParams(vmem_limit_bytes=1024 * 1024),
        )(*results)

    return jax.shard_map(
        on_device,
        mesh=mesh,
        in_specs=(
            P("section", "seq", None),
            P("section", "seq", None),
            P("section", "seq", None),
            P("section", "seq", None),
            P("section", None),
            P("seq", None),
        ),
        out_specs=(P("section", "seq", None), P("section", "seq", None), P("section", "seq", None)),
        check_vma=False,
    )
```

```python
import math

import jax
import jax.numpy as jnp
from jax import lax
from jax.experimental import pallas as pl
from jax.experimental.pallas import tpu as pltpu
from jax.sharding import PartitionSpec as P

MESH = pl.DeviceIdType.MESH
HD = 128
ROWS = 128
HALF = ROWS // 2
SQUARE = 4
NEG = -1e30
F32 = jnp.float32
BF16 = jnp.bfloat16
VMEM_LIMIT = 48 * 1024 * 1024
SIDE = 8
DIRS = 4
PAR = (0, 1, 0, 1)


def dot(a, b, dims):
    return lax.dot_general(a, b, (dims, ((), ())), preferred_element_type=F32)


def kernel(
    heads,
    groups,
    rand,
    gain_in,
    stream,
    cotangent,
    keys,
    values,
    stream_out,
    key_out,
    value_out,
    gain,
    hidden,
    upstream,
    queries,
    grad_query,
    handed,
    arrived,
    hidden_after,
    mean_out,
    mean_in,
    products,
    blocks,
    corner,
    halo,
    slot_keys,
    slot_values,
    terms,
    far_out,
    far_in,
    far_in2,
    mid_out,
    mid_in,
    near_out,
    near_in,
    edge_out,
    edge_in,
    global_out,
    global_in,
    line_sum,
    line_out,
    cross_in,
    cross_out,
    last_in,
    local_sem,
    kv_send,
    kv_recv,
    halo_send,
    halo_recv,
    corner_send,
    corner_recv,
    ret_send,
    ret_recv,
    edge_send,
    edge_recv,
    global_send,
    global_recv,
    cross_send,
    cross_recv,
    last_send,
    last_recv,
    handed_send,
    handed_recv,
    hidden_sem,
    mean_sem,
):
    device = lax.axis_index("seq")
    section = lax.axis_index("section")
    sections = lax.axis_size("section")
    z, y = device // SIDE, device % SIDE
    wanted = rand[0, 0]
    pieces = 2 * groups
    per_group = heads // groups
    factor = HD ** (-0.5)
    edge = (y == 0) | (y == SIDE - 1)

    def at(direction, distance):
        if direction == 0:
            return z * SIDE + (y + distance) % SIDE
        if direction == 1:
            return z * SIDE + (y + SIDE - distance) % SIDE
        if direction == 2:
            return ((z + distance) % SIDE) * SIDE + y
        return ((z + SIDE - distance) % SIDE) * SIDE + y

    def remote(src, dst, send, recv, to):
        return pltpu.make_async_remote_copy(
            src_ref=src,
            dst_ref=dst,
            send_sem=send,
            recv_sem=recv,
            device_id={"seq": to},
            device_id_type=MESH,
        )

    def each(low, high, body):
        def step(i, carry):
            body(i)
            return carry

        lax.fori_loop(low, high, step, 0)

    own = []
    for g in range(groups):
        columns = pl.ds(g * HD, HD)
        own.append(pltpu.make_async_copy(keys.at[0, :, columns], blocks.at[0, 2 * g], local_sem.at[2 * g]))
        own.append(
            pltpu.make_async_copy(values.at[0, :, columns], blocks.at[0, 2 * g + 1], local_sem.at[2 * g + 1])
        )
    for copy in own:
        copy.start()
    load_gain = pltpu.make_async_copy(gain_in, gain, local_sem.at[pieces])
    load_hidden = pltpu.make_async_copy(stream.at[0], hidden, local_sem.at[pieces + 1])
    load_upstream = pltpu.make_async_copy(cotangent.at[0], upstream, local_sem.at[pieces + 2])
    load_gain.start()
    load_hidden.start()
    load_upstream.start()

    barrier = pltpu.get_barrier_semaphore()

    def greet(k):
        pl.semaphore_signal(barrier, inc=1, device_id={"seq": at(0, k)}, device_id_type=MESH)
        pl.semaphore_signal(barrier, inc=1, device_id={"seq": at(2, k)}, device_id_type=MESH)

    each(1, SIDE, greet)
    before = (section + sections - 1) % sections
    after = (section + 1) % sections
    pl.semaphore_signal(barrier, inc=1, device_id={"section": before}, device_id_type=MESH)
    pl.semaphore_signal(barrier, inc=1, device_id={"section": after}, device_id_type=MESH)
    for copy in own:
        copy.wait()
    pl.semaphore_wait(barrier, 2 * (SIDE - 1) + 2)

    line = (z, y)
    cross = (y, z)
    along = (2, 0)
    across = (0, 2)

    def corner_copy(stage, half, i, to, index):
        if stage == 0:
            src = blocks.at[0, 2 * (i // 2) + half, pl.ds((i % 2) * HALF, HALF)]
        else:
            src = corner.at[half, i]
        return remote(
            src, corner.at[half, i], corner_send.at[stage, half, index], corner_recv.at[half, i], to
        )

    @pl.when(device == 0)
    def _():
        corner[0, 0] = blocks[0, 0, :HALF]
        corner[1, 0] = blocks[0, 1, :HALF]

        def scatter(i):
            for half in range(2):
                corner_copy(0, half, i, at(along[half], i), i).start()

        each(1, SIDE, scatter)

    def slot(direction, step):
        return (step, SIDE - step, SIDE + step, 2 * SIDE - step)[direction]

    def both_halves(condition, direction, step, g, act):
        if condition is None:
            act(direction, step, g, step <= 2)
            return

        @pl.when(condition)
        def _():
            act(direction, step, g, True)

        @pl.when(jnp.logical_not(condition))
        def _():
            act(direction, step, g, False)

    def middle(i):
        return (i % SQUARE == 1) | (i % SQUARE == 2)

    def kv_whole(direction, step, sender):
        if step > 2:
            return None
        if step == 2:
            if sender:
                return middle(y if direction < 2 else z)
            return middle((y + SIDE - 1, y + 1, z + SIDE - 1, z + 1)[direction])
        if direction == 0:
            return y != (SIDE - 1 if sender else 0)
        if direction == 1:
            return y != (0 if sender else SIDE - 1)
        if direction == 2:
            return (z % SQUARE != (3 if sender else 0)) | (y == SIDE - 1)
        return (z % SQUARE != (0 if sender else 3)) | (y == 0)

    def kv(direction, step, g, whole):
        part = pl.ds(2 * g, 2) if whole else pl.ds(2 * g + PAR[direction], 1)
        src = blocks.at[0 if step == 1 else slot(direction, step - 1), part]
        return remote(
            src,
            blocks.at[slot(direction, step), part],
            kv_send.at[direction, step - 1, g],
            kv_recv.at[direction, step - 1, g],
            at(direction, 1),
        )

    def kv_start(*what):
        kv(*what).start()

    def kv_arrived(*what):
        kv(*what).wait_recv()

    def kv_left(*what):
        kv(*what).wait_send()

    def halo_copy(g, source, to):
        part = pl.ds(2 * g, 2)
        return remote(blocks.at[source, part], halo.at[part], halo_send.at[g], halo_recv.at[g], to)

    def forward(step, g):
        for direction in range(DIRS):
            if step > 1:
                both_halves(kv_whole(direction, step - 1, False), direction, step - 1, g, kv_arrived)
            both_halves(kv_whole(direction, step, True), direction, step, g, kv_start)
        if step == 2:

            @pl.when(y == SIDE - 1)
            def _():
                halo_copy(g, SIDE + 1, z * SIDE).start()

            @pl.when(y == 0)
            def _():
                halo_copy(g, 2 * SIDE - 1, z * SIDE + SIDE - 1).start()

    each(0, groups, lambda g: forward(1, g))

    hidden_copy = pltpu.make_async_remote_copy(
        src_ref=stream.at[0],
        dst_ref=hidden_after,
        send_sem=hidden_sem.at[0],
        recv_sem=hidden_sem.at[1],
        device_id={"section": before},
        device_id_type=MESH,
    )
    hidden_copy.start()

    load_hidden.wait()

    def square(h, total):
        x = hidden[:, pl.ds(pl.multiple_of(h * HD, HD), HD)].astype(F32)
        return total + x * x

    squares = lax.fori_loop(0, heads, square, jnp.zeros((ROWS, HD), F32))
    inverse = lax.rsqrt(jnp.sum(squares, axis=1, keepdims=True) / (heads * HD) + 1e-05)
    load_gain.wait()

    def query(h):
        columns = pl.ds(pl.multiple_of(h * HD, HD), HD)
        normed = hidden[:, columns].astype(F32) * inverse
        queries[:, columns] = (normed * gain[:, columns]).astype(BF16)

    each(0, heads, query)
    products[...] = jnp.zeros_like(products)

    forward(2, 0)
    forward(2, 1)

    for half in range(2):

        @pl.when(cross[half] == 0)
        def _():
            @pl.when(line[half] != 0)
            def _():
                corner_copy(1, half, line[half], device, 0).wait_recv()

            def spread(k):
                corner_copy(1, half, line[half], at(across[half], k), k).start()

            each(1, SIDE, spread)

    forward(2, 2)
    forward(3, 0)
    forward(2, 3)

    for half in range(2):

        @pl.when(cross[half] != 0)
        def _():
            corner_copy(2, half, line[half], device, 0).wait_recv()

    def over_lines(k):
        for half in range(2):
            corner_copy(2, half, line[half], at(along[half], k), k).start()

    each(1, SIDE, over_lines)
    forward(3, 1)
    forward(3, 2)
    forward(4, 0)
    forward(3, 3)
    forward(4, 1)
    forward(4, 2)
    load_upstream.wait()

    def collect(g):
        for direction in range(DIRS):
            kv(direction, 4, g, False).wait_recv()

        @pl.when(edge)
        def _():
            halo_copy(g, 0, device).wait_recv()

        for half in range(2):
            for i in range(2):

                @pl.when(line[half] != 2 * g + i)
                def _():
                    corner_copy(2, half, 2 * g + i, device, 0).wait_recv()

    partners = (
        (y + 2 - 4 * ((y // 2) % 2), None),
        ((y + 4) % SIDE, None),
        (None, z + 1 - 2 * (z % 2)),
        (None, z + 2 - 4 * ((z // 2) % 2)),
        (None, (z + 4) % SIDE),
    )

    def assemble(g):
        for half, target in ((0, slot_keys), (1, slot_values)):
            piece = 2 * g + half
            target[g, pl.ds(0, ROWS)] = jnp.where(y == 0, halo[piece], blocks[1, piece])
            target[g, pl.ds(ROWS, ROWS)] = blocks[0, piece]
            target[g, pl.ds(2 * ROWS, ROWS)] = jnp.where(
                y == SIDE - 1, halo[piece], blocks[SIDE - 1, piece]
            )
            for i in range(2):
                target[g, pl.ds(3 * ROWS + i * HALF, HALF)] = corner[half, 2 * g + i]
            picked = None
            for to_y, to_z in partners:
                if to_z is None:
                    name, place = z * SIDE + to_y, (y + SIDE - to_y) % SIDE
                else:
                    name, place = to_z * SIDE + y, SIDE + (z + SIDE - to_z) % SIDE
                block = blocks[place, piece]
                picked = block if picked is None else jnp.where(wanted == name, block, picked)
            target[g, pl.ds(4 * ROWS, ROWS)] = picked

    no_before = jnp.where(device == 0, NEG, 0.0).astype(F32)
    no_after = jnp.where(device == SIDE * SIDE - 1, NEG, 0.0).astype(F32)
    bias = (no_before, None, no_after, no_before, None)
    scale = factor * math.log2(math.e)

    def unit(g, first_head, count, fresh):
        columns = [pl.ds(pl.multiple_of((first_head + i) * HD, HD), HD) for i in range(count)]
        q = jnp.concatenate([queries[:, c] for c in columns], axis=0)
        do = jnp.concatenate([upstream[:, c] for c in columns], axis=0)
        k, v = slot_keys[g], slot_values[g]
        raw = dot(k, q, ((1,), (1,)))
        grad_weights = dot(v, do, ((1,), (1,)))
        scores = []
        for i in range(5):
            part = raw[i * ROWS : (i + 1) * ROWS] * scale
            scores.append(part if bias[i] is None else part + bias[i])
        scores = jnp.concatenate(scores, axis=0)
        peak = jnp.max(scores, axis=0, keepdims=True)
        raised = jnp.exp2(scores - peak)
        share = 1.0 / jnp.sum(raised, axis=0, keepdims=True)
        row_dot = jnp.sum(raised * grad_weights, axis=0, keepdims=True) * share
        grad_low = ((raised * (share * factor)) * (grad_weights - row_dot)).astype(BF16)
        weights_low = (raised * share).astype(BF16)
        key_terms = dot(grad_low, q, ((1,), (0,)))
        value_terms = dot(weights_low, do, ((1,), (0,)))
        if fresh:
            terms[2 * g] = key_terms
            terms[2 * g + 1] = value_terms
        else:
            terms[2 * g] += key_terms
            terms[2 * g + 1] += value_terms
        back = dot(grad_low, k, ((0,), (0,)))
        for i, c in enumerate(columns):
            grad_query[:, c] = back[i * ROWS : (i + 1) * ROWS]

    def mark(to):
        return jnp.where(wanted == to, 1.0, 0.0).astype(F32)

    before_rows, own_rows, after_rows, global_rows, random_rows = (
        pl.ds(i * ROWS, ROWS) for i in range(5)
    )

    def ret_whole(direction, step, sender):
        if step > 2:
            return None
        if step == 2:
            i = y if direction < 2 else z
            if not sender:
                i = i + (SIDE - 1, 1, SIDE - 1, 1)[direction]
            low = (i % SQUARE) < 2
            return low if direction in (0, 2) else jnp.logical_not(low)
        if direction == 0:
            return y != (SIDE - 1 if sender else 0)
        if direction == 1:
            return y != (0 if sender else SIDE - 1)
        if direction == 2:
            return (z % SQUARE != (3 if sender else 0)) | (y == 0)
        return (z % SQUARE != (0 if sender else 3)) | (y == SIDE - 1)

    def ret(direction, step, g, whole):
        pair = {4: (far_out, far_in), 3: (far_in, far_in2), 2: (mid_out, mid_in), 1: (near_out, near_in)}
        src, dst = pair[step]
        if step > 2:
            src, dst = src.at[direction, g], dst.at[direction, g]
        else:
            part = pl.ds(0, 2) if whole else pl.ds(PAR[direction], 1)
            src, dst = src.at[direction, g, part], dst.at[direction, g, part]
        return remote(
            src,
            dst,
            ret_send.at[direction, step - 1, g],
            ret_recv.at[direction, step - 1, g],
            at(direction, 1),
        )

    def ret_start(direction, step, g):
        def start(*what):
            ret(*what).start()

        both_halves(ret_whole(direction, step, True), direction, step, g, start)

    def ret_arrived(direction, step, g):
        def wait(*what):
            ret(*what).wait_recv()

        both_halves(ret_whole(direction, step, False), direction, step, g, wait)

    def ret_left(*what):
        ret(*what).wait_send()

    def received(buffer, direction, step, g, half):
        value = buffer[direction, g, half].astype(F32)
        if half == PAR[direction]:
            return value
        return jnp.where(ret_whole(direction, step, False), value, 0.0)

    def global_copy(half, i, source, to):
        return remote(
            global_out.at[half, i],
            global_in.at[half, source],
            global_send.at[half, i],
            global_recv.at[half, source],
            to,
        )

    def edge_copy(g, to):
        part = pl.ds(2 * g, 2)
        return remote(edge_out.at[part], edge_in.at[part], edge_send.at[g], edge_recv.at[g], to)

    def cross_copy(src, dst, send, recv, half, source, to):
        return remote(src.at[half], dst.at[half, source], send.at[half], recv.at[half, source], to)

    def half_rows(i):
        return pl.ds(pl.multiple_of(3 * ROWS + (i % 2) * HALF, HALF), HALF)

    def send_far(g):
        for half in range(2):
            for j in range(2):
                i = 2 * g + j
                global_out[half, i] = terms[2 * g + half, pl.ds(3 * ROWS + j * HALF, HALF)].astype(BF16)

                @pl.when(line[half] != i)
                def _():
                    to = i * SIDE + y if half == 0 else z * SIDE + i
                    global_copy(half, i, line[half], to).start()

        for direction in range(DIRS):
            random = terms[2 * g + PAR[direction], random_rows]
            far_out[direction, g] = (random * mark(at(direction, 4))).astype(BF16)
            ret_start(direction, 4, g)

        @pl.when(y == SIDE - 1)
        def _():
            for half in range(2):
                edge_out[2 * g + half] = terms[2 * g + half, after_rows].astype(BF16)
            edge_copy(g, z * SIDE).start()

        @pl.when(y == 0)
        def _():
            for half in range(2):
                edge_out[2 * g + half] = terms[2 * g + half, before_rows].astype(BF16)
            edge_copy(g, z * SIDE + SIDE - 1).start()

    def pass_far(g):
        for direction in range(DIRS):
            ret_arrived(direction, 4, g)
            ret_start(direction, 3, g)

    def send_mid(g):
        for direction in range(DIRS):
            ret_arrived(direction, 3, g)
            here = mark(at(direction, 2))
            half = PAR[direction]
            mid_out[direction, g, half] = (
                terms[2 * g + half, random_rows] * here + far_in2[direction, g].astype(F32)
            ).astype(BF16)
            mid_out[direction, g, 1 - half] = (terms[2 * g + 1 - half, random_rows] * here).astype(BF16)
            ret_start(direction, 2, g)

    def send_near(g):
        @pl.when(edge)
        def _():
            edge_copy(g, device).wait_recv()

        for direction in range(DIRS):
            ret_arrived(direction, 2, g)
            for half in range(2):
                p = 2 * g + half
                passed = received(mid_in, direction, 2, g, half)
                if direction < 2:
                    rows = after_rows if direction == 0 else before_rows
                    added = jnp.where(
                        y == (SIDE - 1 if direction == 0 else 0),
                        0.0,
                        terms[p, rows].astype(BF16).astype(F32),
                    )
                else:
                    added = terms[p, random_rows] * mark(at(direction, 1)) + jnp.where(
                        y == (0 if direction == 2 else SIDE - 1), edge_in[p].astype(F32), 0.0
                    )
                near_out[direction, g, half] = (passed + added).astype(BF16)
            ret_start(direction, 1, g)

    def to_before(src, dst, send, recv):
        return pltpu.make_async_remote_copy(
            src_ref=src,
            dst_ref=dst,
            send_sem=send,
            recv_sem=recv,
            device_id={"section": before},
            device_id_type=MESH,
        )

    def hand_copy(part):
        columns = pl.ds(pl.multiple_of(part * (per_group * HD), per_group * HD), per_group * HD)
        return to_before(
            handed.at[:, columns], arrived.at[:, columns], handed_send.at[part], handed_recv.at[part]
        )

    def mean_copy():
        return to_before(mean_out, mean_in, mean_sem.at[0], mean_sem.at[1])

    def hand(first_head, count):
        total = products[...]
        for i in range(count):
            columns = pl.ds(pl.multiple_of((first_head + i) * HD, HD), HD)
            grad_norm = grad_query[:, columns] * gain[:, columns]
            total = total + grad_norm * (hidden[:, columns].astype(F32) * inverse)
            handed[:, columns] = (upstream[:, columns].astype(F32) + inverse * grad_norm).astype(BF16)
        products[...] = total

    half_group = per_group // 2

    def group_step(g):
        collect(g)
        assemble(g)
        unit(g, g * per_group, half_group, True)


        @pl.when(g == 0)
        def _():
            forward(4, 3)

        hand(g * per_group, half_group)
        unit(g, g * per_group + half_group, half_group, False)

        send_far(g)
        hand(g * per_group + half_group, half_group)
        hand_copy(g).start()

        @pl.when(g >= 1)
        def _():
            pass_far(g - 1)

        @pl.when(g >= 2)
        def _():
            send_mid(g - 2)

        @pl.when(g >= 3)
        def _():
            send_near(g - 3)

    each(0, groups, group_step)

    mean = jnp.sum(products[...], axis=1, keepdims=True) / (heads * HD)
    mean_out[...] = jnp.broadcast_to(inverse * inverse * mean, (ROWS, HD))
    mean_copy().start()

    def add_crosses():
        for half in range(2):

            @pl.when(cross[half] == 0)
            def _():
                def add_cross(k, total):
                    cross_copy(line_out, cross_in, cross_send, cross_recv, half, k, device).wait_recv()
                    return total + cross_in[half, k].astype(F32)

                line_sum[half] = lax.fori_loop(1, SIDE, add_cross, line_sum[half])

                @pl.when(line[half] != 0)
                def _():
                    cross_out[half] = line_sum[half].astype(BF16)
                    cross_copy(cross_out, last_in, last_send, last_recv, half, line[half], 0).start()

    def receive_hand():
        hidden_copy.wait_recv()
        mean_copy().wait_recv()
        for part in range(groups):
            hand_copy(part).wait_recv()

        def finish(h):
            columns = pl.ds(pl.multiple_of(h * HD, HD), HD)
            along_input = hidden_after[:, columns].astype(F32) * mean_in[...]
            stream_out[0, :, columns] = (arrived[:, columns].astype(F32) - along_input).astype(BF16)

        each(0, heads, finish)

    for g in range(1, groups):
        if g == 1:
            pass_far(3)
        if g <= 2:
            send_mid(g + 1)
        if g == 3:
            receive_hand()
            add_crosses()
        send_near(g)
        if g == 1:
            for half in range(2):
                start = terms[2 * (line[half] // 2) + half, half_rows(line[half])]

                def add_line(k, total):
                    source = (line[half] + k) % SIDE
                    global_copy(half, 0, source, device).wait_recv()
                    return total + global_in[half, source].astype(F32)

                line_sum[half] = lax.fori_loop(1, SIDE, add_line, start)

                @pl.when(cross[half] != 0)
                def _():
                    line_out[half] = line_sum[half].astype(BF16)
                    to = z * SIDE if half == 0 else y
                    cross_copy(line_out, cross_in, cross_send, cross_recv, half, cross[half], to).start()

    @pl.when(device == 0)
    def _():
        for half in range(2):

            def take(i):
                cross_copy(cross_out, last_in, last_send, last_recv, half, i, device).wait_recv()
                rows = pl.ds(pl.multiple_of(ROWS + (i % 2) * HALF, HALF), HALF)
                terms[2 * (i // 2) + half, rows] += last_in[half, i].astype(F32)

            each(1, SIDE, take)
            terms[half, pl.ds(ROWS, HALF)] += line_sum[half]

    for g in range(groups):
        for direction in range(DIRS):
            ret_arrived(direction, 1, g)
        for half, out in ((0, key_out), (1, value_out)):
            total = terms[2 * g + half, own_rows]
            for direction in range(DIRS):
                total = total + received(near_in, direction, 1, g, half)
            out[0, :, pl.ds(g * HD, HD)] = total.astype(BF16)

    def sent(g):
        for direction in range(DIRS):
            for step in (1, 2, 3, 4):
                both_halves(kv_whole(direction, step, True), direction, step, g, kv_left)
                both_halves(ret_whole(direction, step, True), direction, step, g, ret_left)

        @pl.when(edge)
        def _():
            halo_copy(g, 0, device).wait_send()
            edge_copy(g, device).wait_send()

    each(0, groups, sent)

    for half in range(2):

        def sent_pieces(k):
            corner_copy(2, half, 0, device, k).wait_send()
            global_copy(half, (line[half] + k) % SIDE, 0, device).wait_send()

        each(1, SIDE, sent_pieces)

        @pl.when(cross[half] == 0)
        def _():
            def sent_across(k):
                corner_copy(1, half, 0, device, k).wait_send()

            each(1, SIDE, sent_across)

            @pl.when(line[half] != 0)
            def _():
                cross_copy(cross_out, last_in, last_send, last_recv, half, 0, device).wait_send()

        @pl.when(cross[half] != 0)
        def _():
            cross_copy(line_out, cross_in, cross_send, cross_recv, half, 0, device).wait_send()

    @pl.when(device == 0)
    def _():
        def sent_corner(i):
            for half in range(2):
                corner_copy(0, half, i, device, i).wait_send()

        each(1, SIDE, sent_corner)

    hidden_copy.wait_send()
    mean_copy().wait_send()
    for part in range(groups):
        hand_copy(part).wait_send()


def solution(mesh):
    def on_device(stream, cotangent, keys, values, gain, rand_blocks):
        heads = stream.shape[2] // HD
        groups = keys.shape[2] // HD
        pieces = 2 * groups
        block = (ROWS, HD)
        part = (HALF, HD)
        vmem = pl.BlockSpec(memory_space=pltpu.VMEM)
        hbm = pl.BlockSpec(memory_space=pltpu.HBM)
        dma = pltpu.SemaphoreType.DMA

        def bf16(*shape):
            return pltpu.VMEM(shape, BF16)

        def f32(*shape):
            return pltpu.VMEM(shape, F32)

        def in_hbm(array):
            return pltpu.with_memory_space_constraint(array, pltpu.HBM)

        def body(*refs):
            kernel(heads, groups, *refs)

        results = pl.pallas_call(
            body,
            name="relay",
            out_shape=(
                jax.ShapeDtypeStruct(stream.shape, BF16),
                jax.ShapeDtypeStruct(keys.shape, BF16),
                jax.ShapeDtypeStruct(values.shape, BF16),
            ),
            in_specs=[pl.BlockSpec(memory_space=pltpu.SMEM), hbm, hbm, hbm, hbm, hbm],
            out_specs=(vmem, vmem, vmem),
            scratch_shapes=[
                f32(1, heads * HD),
                bf16(ROWS, heads * HD),
                bf16(ROWS, heads * HD),
                bf16(ROWS, heads * HD),
                f32(ROWS, heads * HD),
                bf16(ROWS, heads * HD),
                bf16(ROWS, heads * HD),
                bf16(ROWS, heads * HD),
                f32(*block),
                f32(*block),
                f32(*block),
                bf16(2 * SIDE, pieces, *block),
                bf16(2, SIDE, *part),
                bf16(pieces, *block),
                bf16(groups, 5 * ROWS, HD),
                bf16(groups, 5 * ROWS, HD),
                f32(pieces, 5 * ROWS, HD),
                bf16(DIRS, groups, *block),
                bf16(DIRS, groups, *block),
                bf16(DIRS, groups, *block),
                bf16(DIRS, groups, 2, *block),
                bf16(DIRS, groups, 2, *block),
                bf16(DIRS, groups, 2, *block),
                bf16(DIRS, groups, 2, *block),
                bf16(pieces, *block),
                bf16(pieces, *block),
                bf16(2, SIDE, *part),
                bf16(2, SIDE, *part),
                f32(2, *part),
                bf16(2, *part),
                bf16(2, SIDE, *part),
                bf16(2, *part),
                bf16(2, SIDE, *part),
                dma((pieces + 3,)),
                dma((DIRS, 4, groups)),
                dma((DIRS, 4, groups)),
                dma((groups,)),
                dma((groups,)),
                dma((3, 2, SIDE)),
                dma((2, SIDE)),
                dma((DIRS, 4, groups)),
                dma((DIRS, 4, groups)),
                dma((groups,)),
                dma((groups,)),
                dma((2, SIDE)),
                dma((2, SIDE)),
                dma((2,)),
                dma((2, SIDE)),
                dma((2,)),
                dma((2, SIDE)),
                dma((groups,)),
                dma((groups,)),
                dma((2,)),
                dma((2,)),
            ],
            compiler_params=pltpu.CompilerParams(
                collective_id=0, has_side_effects=True, vmem_limit_bytes=VMEM_LIMIT
            ),
        )(rand_blocks, *(in_hbm(a) for a in (gain, stream, cotangent, keys, values)))

        def write(*refs):
            sources, targets, sems = refs[:3], refs[3:6], refs[6]
            copies = [
                pltpu.make_async_copy(src, dst, sems.at[i])
                for i, (src, dst) in enumerate(zip(sources, targets))
            ]
            for copy in copies:
                copy.start()
            for copy in copies:
                copy.wait()

        return pl.pallas_call(
            write,
            name="write",
            out_shape=tuple(jax.ShapeDtypeStruct(r.shape, r.dtype) for r in results),
            in_specs=[pl.BlockSpec(memory_space=pl.ANY)] * 3,
            out_specs=(hbm,) * 3,
            scratch_shapes=[dma((3,))],
            compiler_params=pltpu.CompilerParams(vmem_limit_bytes=1024 * 1024),
        )(*results)

    return jax.shard_map(
        on_device,
        mesh=mesh,
        in_specs=(
            P("section", "seq", None),
            P("section", "seq", None),
            P("section", "seq", None),
            P("section", "seq", None),
            P("section", None),
            P("seq", None),
        ),
        out_specs=(P("section", "seq", None), P("section", "seq", None), P("section", "seq", None)),
        check_vma=False,
    )
```

```python
import math

import jax
import jax.numpy as jnp
from jax import lax
from jax.experimental import pallas as pl
from jax.experimental.pallas import tpu as pltpu
from jax.sharding import PartitionSpec as P

MESH = pl.DeviceIdType.MESH
HD = 128
ROWS = 128
HALF = ROWS // 2
SQUARE = 4
NEG = -1e30
F32 = jnp.float32
BF16 = jnp.bfloat16
VMEM_LIMIT = 48 * 1024 * 1024
SIDE = 8
DIRS = 4
PAR = (0, 1, 0, 1)


def dot(a, b, dims):
    return lax.dot_general(a, b, (dims, ((), ())), preferred_element_type=F32)


def kernel(
    heads,
    groups,
    rand,
    gain_in,
    stream,
    cotangent,
    keys,
    values,
    stream_out,
    key_out,
    value_out,
    gain,
    hidden,
    upstream,
    queries,
    grad_query,
    handed,
    arrived,
    hidden_after,
    mean_out,
    mean_in,
    products,
    blocks,
    corner,
    halo,
    slot_keys,
    slot_values,
    terms,
    far_out,
    far_in,
    far_in2,
    mid_out,
    mid_in,
    near_out,
    near_in,
    edge_out,
    edge_in,
    global_out,
    global_in,
    line_sum,
    line_out,
    cross_in,
    cross_out,
    last_in,
    local_sem,
    kv_send,
    kv_recv,
    halo_send,
    halo_recv,
    corner_send,
    corner_recv,
    ret_send,
    ret_recv,
    edge_send,
    edge_recv,
    global_send,
    global_recv,
    cross_send,
    cross_recv,
    last_send,
    last_recv,
    handed_send,
    handed_recv,
    hidden_sem,
    mean_sem,
):
    device = lax.axis_index("seq")
    section = lax.axis_index("section")
    sections = lax.axis_size("section")
    z, y = device // SIDE, device % SIDE
    wanted = rand[0, 0]
    pieces = 2 * groups
    per_group = heads // groups
    factor = HD ** (-0.5)
    edge = (y == 0) | (y == SIDE - 1)

    def at(direction, distance):
        if direction == 0:
            return z * SIDE + (y + distance) % SIDE
        if direction == 1:
            return z * SIDE + (y + SIDE - distance) % SIDE
        if direction == 2:
            return ((z + distance) % SIDE) * SIDE + y
        return ((z + SIDE - distance) % SIDE) * SIDE + y

    def remote(src, dst, send, recv, to):
        return pltpu.make_async_remote_copy(
            src_ref=src,
            dst_ref=dst,
            send_sem=send,
            recv_sem=recv,
            device_id={"seq": to},
            device_id_type=MESH,
        )

    def each(low, high, body):
        def step(i, carry):
            body(i)
            return carry

        lax.fori_loop(low, high, step, 0)

    own = []
    for g in range(groups):
        columns = pl.ds(g * HD, HD)
        own.append(pltpu.make_async_copy(keys.at[0, :, columns], blocks.at[0, 2 * g], local_sem.at[2 * g]))
        own.append(
            pltpu.make_async_copy(values.at[0, :, columns], blocks.at[0, 2 * g + 1], local_sem.at[2 * g + 1])
        )
    for copy in own:
        copy.start()
    load_gain = pltpu.make_async_copy(gain_in, gain, local_sem.at[pieces])
    load_hidden = pltpu.make_async_copy(stream.at[0], hidden, local_sem.at[pieces + 1])
    load_upstream = pltpu.make_async_copy(cotangent.at[0], upstream, local_sem.at[pieces + 2])
    load_gain.start()
    load_hidden.start()
    load_upstream.start()

    barrier = pltpu.get_barrier_semaphore()

    def greet(k):
        pl.semaphore_signal(barrier, inc=1, device_id={"seq": at(0, k)}, device_id_type=MESH)
        pl.semaphore_signal(barrier, inc=1, device_id={"seq": at(2, k)}, device_id_type=MESH)

    each(1, SIDE, greet)
    before = (section + sections - 1) % sections
    after = (section + 1) % sections
    pl.semaphore_signal(barrier, inc=1, device_id={"section": before}, device_id_type=MESH)
    pl.semaphore_signal(barrier, inc=1, device_id={"section": after}, device_id_type=MESH)
    for copy in own:
        copy.wait()
    pl.semaphore_wait(barrier, 2 * (SIDE - 1) + 2)

    line = (z, y)
    cross = (y, z)
    along = (2, 0)
    across = (0, 2)

    def corner_copy(stage, half, i, to, index):
        if stage == 0:
            src = blocks.at[0, 2 * (i // 2) + half, pl.ds((i % 2) * HALF, HALF)]
        else:
            src = corner.at[half, i]
        return remote(
            src, corner.at[half, i], corner_send.at[stage, half, index], corner_recv.at[half, i], to
        )

    @pl.when(device == 0)
    def _():
        corner[0, 0] = blocks[0, 0, :HALF]
        corner[1, 0] = blocks[0, 1, :HALF]

        def scatter(i):
            for half in range(2):
                corner_copy(0, half, i, at(along[half], i), i).start()

        each(1, SIDE, scatter)

    def slot(direction, step):
        return (step, SIDE - step, SIDE + step, 2 * SIDE - step)[direction]

    def both_halves(condition, direction, step, g, act):
        if condition is None:
            act(direction, step, g, step <= 2)
            return

        @pl.when(condition)
        def _():
            act(direction, step, g, True)

        @pl.when(jnp.logical_not(condition))
        def _():
            act(direction, step, g, False)

    def middle(i):
        return (i % SQUARE == 1) | (i % SQUARE == 2)

    def kv_whole(direction, step, sender):
        if step > 2:
            return None
        if step == 2:
            if sender:
                return middle(y if direction < 2 else z)
            return middle((y + SIDE - 1, y + 1, z + SIDE - 1, z + 1)[direction])
        if direction == 0:
            return y != (SIDE - 1 if sender else 0)
        if direction == 1:
            return y != (0 if sender else SIDE - 1)
        if direction == 2:
            return (z % SQUARE != (3 if sender else 0)) | (y == SIDE - 1)
        return (z % SQUARE != (0 if sender else 3)) | (y == 0)

    def kv(direction, step, g, whole):
        part = pl.ds(2 * g, 2) if whole else pl.ds(2 * g + PAR[direction], 1)
        src = blocks.at[0 if step == 1 else slot(direction, step - 1), part]
        return remote(
            src,
            blocks.at[slot(direction, step), part],
            kv_send.at[direction, step - 1, g],
            kv_recv.at[direction, step - 1, g],
            at(direction, 1),
        )

    def kv_start(*what):
        kv(*what).start()

    def kv_arrived(*what):
        kv(*what).wait_recv()

    def kv_left(*what):
        kv(*what).wait_send()

    def halo_copy(g, source, to):
        part = pl.ds(2 * g, 2)
        return remote(blocks.at[source, part], halo.at[part], halo_send.at[g], halo_recv.at[g], to)

    def forward(step, g):
        for direction in range(DIRS):
            if step > 1:
                both_halves(kv_whole(direction, step - 1, False), direction, step - 1, g, kv_arrived)
            both_halves(kv_whole(direction, step, True), direction, step, g, kv_start)
        if step == 2:

            @pl.when(y == SIDE - 1)
            def _():
                halo_copy(g, SIDE + 1, z * SIDE).start()

            @pl.when(y == 0)
            def _():
                halo_copy(g, 2 * SIDE - 1, z * SIDE + SIDE - 1).start()

    each(0, groups, lambda g: forward(1, g))

    hidden_copy = pltpu.make_async_remote_copy(
        src_ref=stream.at[0],
        dst_ref=hidden_after,
        send_sem=hidden_sem.at[0],
        recv_sem=hidden_sem.at[1],
        device_id={"section": before},
        device_id_type=MESH,
    )
    hidden_copy.start()

    load_hidden.wait()

    def square(h, total):
        x = hidden[:, pl.ds(pl.multiple_of(h * HD, HD), HD)].astype(F32)
        return total + x * x

    squares = lax.fori_loop(0, heads, square, jnp.zeros((ROWS, HD), F32))
    inverse = lax.rsqrt(jnp.sum(squares, axis=1, keepdims=True) / (heads * HD) + 1e-05)
    load_gain.wait()

    def query(h):
        columns = pl.ds(pl.multiple_of(h * HD, HD), HD)
        normed = hidden[:, columns].astype(F32) * inverse
        queries[:, columns] = (normed * gain[:, columns]).astype(BF16)

    each(0, heads, query)
    products[...] = jnp.zeros_like(products)

    forward(2, 0)
    forward(2, 1)

    for half in range(2):

        @pl.when(cross[half] == 0)
        def _():
            @pl.when(line[half] != 0)
            def _():
                corner_copy(1, half, line[half], device, 0).wait_recv()

            def spread(k):
                corner_copy(1, half, line[half], at(across[half], k), k).start()

            each(1, SIDE, spread)

    forward(2, 2)
    forward(3, 0)
    forward(2, 3)

    for half in range(2):

        @pl.when(cross[half] != 0)
        def _():
            corner_copy(2, half, line[half], device, 0).wait_recv()

    def over_lines(k):
        for half in range(2):
            corner_copy(2, half, line[half], at(along[half], k), k).start()

    each(1, SIDE, over_lines)
    forward(3, 1)
    forward(3, 2)
    forward(4, 0)
    forward(3, 3)
    forward(4, 1)
    forward(4, 2)
    load_upstream.wait()

    def collect(g):
        for direction in range(DIRS):
            kv(direction, 4, g, False).wait_recv()

        @pl.when(edge)
        def _():
            halo_copy(g, 0, device).wait_recv()

        for half in range(2):
            for i in range(2):

                @pl.when(line[half] != 2 * g + i)
                def _():
                    corner_copy(2, half, 2 * g + i, device, 0).wait_recv()

    partners = (
        (y + 2 - 4 * ((y // 2) % 2), None),
        ((y + 4) % SIDE, None),
        (None, z + 1 - 2 * (z % 2)),
        (None, z + 2 - 4 * ((z // 2) % 2)),
        (None, (z + 4) % SIDE),
    )

    def assemble(g):
        for half, target in ((0, slot_keys), (1, slot_values)):
            piece = 2 * g + half
            target[g, pl.ds(0, ROWS)] = jnp.where(y == 0, halo[piece], blocks[1, piece])
            target[g, pl.ds(ROWS, ROWS)] = blocks[0, piece]
            target[g, pl.ds(2 * ROWS, ROWS)] = jnp.where(
                y == SIDE - 1, halo[piece], blocks[SIDE - 1, piece]
            )
            for i in range(2):
                target[g, pl.ds(3 * ROWS + i * HALF, HALF)] = corner[half, 2 * g + i]
            picked = None
            for to_y, to_z in partners:
                if to_z is None:
                    name, place = z * SIDE + to_y, (y + SIDE - to_y) % SIDE
                else:
                    name, place = to_z * SIDE + y, SIDE + (z + SIDE - to_z) % SIDE
                block = blocks[place, piece]
                picked = block if picked is None else jnp.where(wanted == name, block, picked)
            target[g, pl.ds(4 * ROWS, ROWS)] = picked

    no_before = jnp.where(device == 0, NEG, 0.0).astype(F32)
    no_after = jnp.where(device == SIDE * SIDE - 1, NEG, 0.0).astype(F32)
    bias = (no_before, None, no_after, no_before, None)
    scale = factor * math.log2(math.e)

    def unit(g, first_head, count):
        columns = [pl.ds(pl.multiple_of((first_head + i) * HD, HD), HD) for i in range(count)]
        q = jnp.concatenate([queries[:, c] for c in columns], axis=0)
        do = jnp.concatenate([upstream[:, c] for c in columns], axis=0)
        k, v = slot_keys[g], slot_values[g]
        raw = dot(k, q, ((1,), (1,)))
        grad_weights = dot(v, do, ((1,), (1,)))
        scores = []
        for i in range(5):
            part = raw[i * ROWS : (i + 1) * ROWS] * scale
            scores.append(part if bias[i] is None else part + bias[i])
        scores = jnp.concatenate(scores, axis=0)
        peak = jnp.max(scores, axis=0, keepdims=True)
        raised = jnp.exp2(scores - peak)
        share = 1.0 / jnp.sum(raised, axis=0, keepdims=True)
        row_dot = jnp.sum(raised * grad_weights, axis=0, keepdims=True) * share
        grad_low = ((raised * (share * factor)) * (grad_weights - row_dot)).astype(BF16)
        weights_low = (raised * share).astype(BF16)
        key_terms = dot(grad_low, q, ((1,), (0,)))
        value_terms = dot(weights_low, do, ((1,), (0,)))
        terms[2 * g] = key_terms
        terms[2 * g + 1] = value_terms
        back = dot(grad_low, k, ((0,), (0,)))
        for i, c in enumerate(columns):
            grad_query[:, c] = back[i * ROWS : (i + 1) * ROWS]

    def mark(to):
        return jnp.where(wanted == to, 1.0, 0.0).astype(F32)

    before_rows, own_rows, after_rows, global_rows, random_rows = (
        pl.ds(i * ROWS, ROWS) for i in range(5)
    )

    def ret_whole(direction, step, sender):
        if step > 2:
            return None
        if step == 2:
            i = y if direction < 2 else z
            if not sender:
                i = i + (SIDE - 1, 1, SIDE - 1, 1)[direction]
            low = (i % SQUARE) < 2
            return low if direction in (0, 2) else jnp.logical_not(low)
        if direction == 0:
            return y != (SIDE - 1 if sender else 0)
        if direction == 1:
            return y != (0 if sender else SIDE - 1)
        if direction == 2:
            return (z % SQUARE != (3 if sender else 0)) | (y == 0)
        return (z % SQUARE != (0 if sender else 3)) | (y == SIDE - 1)

    def ret(direction, step, g, whole):
        pair = {4: (far_out, far_in), 3: (far_in, far_in2), 2: (mid_out, mid_in), 1: (near_out, near_in)}
        src, dst = pair[step]
        if step > 2:
            src, dst = src.at[direction, g], dst.at[direction, g]
        else:
            part = pl.ds(0, 2) if whole else pl.ds(PAR[direction], 1)
            src, dst = src.at[direction, g, part], dst.at[direction, g, part]
        return remote(
            src,
            dst,
            ret_send.at[direction, step - 1, g],
            ret_recv.at[direction, step - 1, g],
            at(direction, 1),
        )

    def ret_start(direction, step, g):
        def start(*what):
            ret(*what).start()

        both_halves(ret_whole(direction, step, True), direction, step, g, start)

    def ret_arrived(direction, step, g):
        def wait(*what):
            ret(*what).wait_recv()

        both_halves(ret_whole(direction, step, False), direction, step, g, wait)

    def ret_left(*what):
        ret(*what).wait_send()

    def received(buffer, direction, step, g, half):
        value = buffer[direction, g, half].astype(F32)
        if half == PAR[direction]:
            return value
        return jnp.where(ret_whole(direction, step, False), value, 0.0)

    def global_copy(half, i, source, to):
        return remote(
            global_out.at[half, i],
            global_in.at[half, source],
            global_send.at[half, i],
            global_recv.at[half, source],
            to,
        )

    def edge_copy(g, to):
        part = pl.ds(2 * g, 2)
        return remote(edge_out.at[part], edge_in.at[part], edge_send.at[g], edge_recv.at[g], to)

    def cross_copy(src, dst, send, recv, half, source, to):
        return remote(src.at[half], dst.at[half, source], send.at[half], recv.at[half, source], to)

    def half_rows(i):
        return pl.ds(pl.multiple_of(3 * ROWS + (i % 2) * HALF, HALF), HALF)

    def send_far(g):
        for half in range(2):
            for j in range(2):
                i = 2 * g + j
                global_out[half, i] = terms[2 * g + half, pl.ds(3 * ROWS + j * HALF, HALF)].astype(BF16)

                @pl.when(line[half] != i)
                def _():
                    to = i * SIDE + y if half == 0 else z * SIDE + i
                    global_copy(half, i, line[half], to).start()

        for direction in range(DIRS):
            random = terms[2 * g + PAR[direction], random_rows]
            far_out[direction, g] = (random * mark(at(direction, 4))).astype(BF16)
            ret_start(direction, 4, g)

        @pl.when(y == SIDE - 1)
        def _():
            for half in range(2):
                edge_out[2 * g + half] = terms[2 * g + half, after_rows].astype(BF16)
            edge_copy(g, z * SIDE).start()

        @pl.when(y == 0)
        def _():
            for half in range(2):
                edge_out[2 * g + half] = terms[2 * g + half, before_rows].astype(BF16)
            edge_copy(g, z * SIDE + SIDE - 1).start()

    def pass_far(g):
        for direction in range(DIRS):
            ret_arrived(direction, 4, g)
            ret_start(direction, 3, g)

    def send_mid(g):
        for direction in range(DIRS):
            ret_arrived(direction, 3, g)
            here = mark(at(direction, 2))
            half = PAR[direction]
            mid_out[direction, g, half] = (
                terms[2 * g + half, random_rows] * here + far_in2[direction, g].astype(F32)
            ).astype(BF16)
            mid_out[direction, g, 1 - half] = (terms[2 * g + 1 - half, random_rows] * here).astype(BF16)
            ret_start(direction, 2, g)

    def send_near(g):
        @pl.when(edge)
        def _():
            edge_copy(g, device).wait_recv()

        for direction in range(DIRS):
            ret_arrived(direction, 2, g)
            for half in range(2):
                p = 2 * g + half
                passed = received(mid_in, direction, 2, g, half)
                if direction < 2:
                    rows = after_rows if direction == 0 else before_rows
                    added = jnp.where(
                        y == (SIDE - 1 if direction == 0 else 0),
                        0.0,
                        terms[p, rows].astype(BF16).astype(F32),
                    )
                else:
                    added = terms[p, random_rows] * mark(at(direction, 1)) + jnp.where(
                        y == (0 if direction == 2 else SIDE - 1), edge_in[p].astype(F32), 0.0
                    )
                near_out[direction, g, half] = (passed + added).astype(BF16)
            ret_start(direction, 1, g)

    def to_before(src, dst, send, recv):
        return pltpu.make_async_remote_copy(
            src_ref=src,
            dst_ref=dst,
            send_sem=send,
            recv_sem=recv,
            device_id={"section": before},
            device_id_type=MESH,
        )

    def hand_copy(part):
        columns = pl.ds(pl.multiple_of(part * (per_group * HD), per_group * HD), per_group * HD)
        return to_before(
            handed.at[:, columns], arrived.at[:, columns], handed_send.at[part], handed_recv.at[part]
        )

    def mean_copy():
        return to_before(mean_out, mean_in, mean_sem.at[0], mean_sem.at[1])

    def hand(first_head, count):
        total = products[...]
        for i in range(count):
            columns = pl.ds(pl.multiple_of((first_head + i) * HD, HD), HD)
            grad_norm = grad_query[:, columns] * gain[:, columns]
            total = total + grad_norm * (hidden[:, columns].astype(F32) * inverse)
            handed[:, columns] = (upstream[:, columns].astype(F32) + inverse * grad_norm).astype(BF16)
        products[...] = total

    def group_step(g):
        collect(g)
        assemble(g)
        unit(g, g * per_group, per_group)


        @pl.when(g == 0)
        def _():
            forward(4, 3)


        send_far(g)

        @pl.when(g >= 1)
        def _():
            pass_far(g - 1)

        @pl.when(g >= 2)
        def _():
            send_mid(g - 2)

        @pl.when(g >= 3)
        def _():
            send_near(g - 3)

        hand(g * per_group, per_group)
        hand_copy(g).start()

    each(0, groups, group_step)

    mean = jnp.sum(products[...], axis=1, keepdims=True) / (heads * HD)
    mean_out[...] = jnp.broadcast_to(inverse * inverse * mean, (ROWS, HD))
    mean_copy().start()

    def add_crosses():
        for half in range(2):

            @pl.when(cross[half] == 0)
            def _():
                def add_cross(k, total):
                    cross_copy(line_out, cross_in, cross_send, cross_recv, half, k, device).wait_recv()
                    return total + cross_in[half, k].astype(F32)

                line_sum[half] = lax.fori_loop(1, SIDE, add_cross, line_sum[half])

                @pl.when(line[half] != 0)
                def _():
                    cross_out[half] = line_sum[half].astype(BF16)
                    cross_copy(cross_out, last_in, last_send, last_recv, half, line[half], 0).start()

    def receive_hand():
        hidden_copy.wait_recv()
        mean_copy().wait_recv()
        for part in range(groups):
            hand_copy(part).wait_recv()

        def finish(h):
            columns = pl.ds(pl.multiple_of(h * HD, HD), HD)
            along_input = hidden_after[:, columns].astype(F32) * mean_in[...]
            stream_out[0, :, columns] = (arrived[:, columns].astype(F32) - along_input).astype(BF16)

        each(0, heads, finish)

    for g in range(1, groups):
        if g == 1:
            pass_far(3)
        if g <= 2:
            send_mid(g + 1)
        if g == 3:
            receive_hand()
            add_crosses()
        if g == 1:
            for half in range(2):
                start = terms[2 * (line[half] // 2) + half, half_rows(line[half])]

                def add_line(k, total):
                    source = (line[half] + k) % SIDE
                    global_copy(half, 0, source, device).wait_recv()
                    return total + global_in[half, source].astype(F32)

                line_sum[half] = lax.fori_loop(1, SIDE, add_line, start)

                @pl.when(cross[half] != 0)
                def _():
                    line_out[half] = line_sum[half].astype(BF16)
                    to = z * SIDE if half == 0 else y
                    cross_copy(line_out, cross_in, cross_send, cross_recv, half, cross[half], to).start()

        send_near(g)

    @pl.when(device == 0)
    def _():
        for half in range(2):

            def take(i):
                cross_copy(cross_out, last_in, last_send, last_recv, half, i, device).wait_recv()
                rows = pl.ds(pl.multiple_of(ROWS + (i % 2) * HALF, HALF), HALF)
                terms[2 * (i // 2) + half, rows] += last_in[half, i].astype(F32)

            each(1, SIDE, take)
            terms[half, pl.ds(ROWS, HALF)] += line_sum[half]

    for g in range(groups):
        for direction in range(DIRS):
            ret_arrived(direction, 1, g)
        for half, out in ((0, key_out), (1, value_out)):
            total = terms[2 * g + half, own_rows]
            for direction in range(DIRS):
                total = total + received(near_in, direction, 1, g, half)
            out[0, :, pl.ds(g * HD, HD)] = total.astype(BF16)

    def sent(g):
        for direction in range(DIRS):
            for step in (1, 2, 3, 4):
                both_halves(kv_whole(direction, step, True), direction, step, g, kv_left)
                both_halves(ret_whole(direction, step, True), direction, step, g, ret_left)

        @pl.when(edge)
        def _():
            halo_copy(g, 0, device).wait_send()
            edge_copy(g, device).wait_send()

    each(0, groups, sent)

    for half in range(2):

        def sent_pieces(k):
            corner_copy(2, half, 0, device, k).wait_send()
            global_copy(half, (line[half] + k) % SIDE, 0, device).wait_send()

        each(1, SIDE, sent_pieces)

        @pl.when(cross[half] == 0)
        def _():
            def sent_across(k):
                corner_copy(1, half, 0, device, k).wait_send()

            each(1, SIDE, sent_across)

            @pl.when(line[half] != 0)
            def _():
                cross_copy(cross_out, last_in, last_send, last_recv, half, 0, device).wait_send()

        @pl.when(cross[half] != 0)
        def _():
            cross_copy(line_out, cross_in, cross_send, cross_recv, half, 0, device).wait_send()

    @pl.when(device == 0)
    def _():
        def sent_corner(i):
            for half in range(2):
                corner_copy(0, half, i, device, i).wait_send()

        each(1, SIDE, sent_corner)

    hidden_copy.wait_send()
    mean_copy().wait_send()
    for part in range(groups):
        hand_copy(part).wait_send()


def solution(mesh):
    def on_device(stream, cotangent, keys, values, gain, rand_blocks):
        heads = stream.shape[2] // HD
        groups = keys.shape[2] // HD
        pieces = 2 * groups
        block = (ROWS, HD)
        part = (HALF, HD)
        vmem = pl.BlockSpec(memory_space=pltpu.VMEM)
        hbm = pl.BlockSpec(memory_space=pltpu.HBM)
        dma = pltpu.SemaphoreType.DMA

        def bf16(*shape):
            return pltpu.VMEM(shape, BF16)

        def f32(*shape):
            return pltpu.VMEM(shape, F32)

        def in_hbm(array):
            return pltpu.with_memory_space_constraint(array, pltpu.HBM)

        def body(*refs):
            kernel(heads, groups, *refs)

        results = pl.pallas_call(
            body,
            name="relay",
            out_shape=(
                jax.ShapeDtypeStruct(stream.shape, BF16),
                jax.ShapeDtypeStruct(keys.shape, BF16),
                jax.ShapeDtypeStruct(values.shape, BF16),
            ),
            in_specs=[pl.BlockSpec(memory_space=pltpu.SMEM), hbm, hbm, hbm, hbm, hbm],
            out_specs=(vmem, vmem, vmem),
            scratch_shapes=[
                f32(1, heads * HD),
                bf16(ROWS, heads * HD),
                bf16(ROWS, heads * HD),
                bf16(ROWS, heads * HD),
                f32(ROWS, heads * HD),
                bf16(ROWS, heads * HD),
                bf16(ROWS, heads * HD),
                bf16(ROWS, heads * HD),
                f32(*block),
                f32(*block),
                f32(*block),
                bf16(2 * SIDE, pieces, *block),
                bf16(2, SIDE, *part),
                bf16(pieces, *block),
                bf16(groups, 5 * ROWS, HD),
                bf16(groups, 5 * ROWS, HD),
                f32(pieces, 5 * ROWS, HD),
                bf16(DIRS, groups, *block),
                bf16(DIRS, groups, *block),
                bf16(DIRS, groups, *block),
                bf16(DIRS, groups, 2, *block),
                bf16(DIRS, groups, 2, *block),
                bf16(DIRS, groups, 2, *block),
                bf16(DIRS, groups, 2, *block),
                bf16(pieces, *block),
                bf16(pieces, *block),
                bf16(2, SIDE, *part),
                bf16(2, SIDE, *part),
                f32(2, *part),
                bf16(2, *part),
                bf16(2, SIDE, *part),
                bf16(2, *part),
                bf16(2, SIDE, *part),
                dma((pieces + 3,)),
                dma((DIRS, 4, groups)),
                dma((DIRS, 4, groups)),
                dma((groups,)),
                dma((groups,)),
                dma((3, 2, SIDE)),
                dma((2, SIDE)),
                dma((DIRS, 4, groups)),
                dma((DIRS, 4, groups)),
                dma((groups,)),
                dma((groups,)),
                dma((2, SIDE)),
                dma((2, SIDE)),
                dma((2,)),
                dma((2, SIDE)),
                dma((2,)),
                dma((2, SIDE)),
                dma((groups,)),
                dma((groups,)),
                dma((2,)),
                dma((2,)),
            ],
            compiler_params=pltpu.CompilerParams(
                collective_id=0, has_side_effects=True, vmem_limit_bytes=VMEM_LIMIT
            ),
        )(rand_blocks, *(in_hbm(a) for a in (gain, stream, cotangent, keys, values)))

        def write(*refs):
            sources, targets, sems = refs[:3], refs[3:6], refs[6]
            copies = [
                pltpu.make_async_copy(src, dst, sems.at[i])
                for i, (src, dst) in enumerate(zip(sources, targets))
            ]
            for copy in copies:
                copy.start()
            for copy in copies:
                copy.wait()

        return pl.pallas_call(
            write,
            name="write",
            out_shape=tuple(jax.ShapeDtypeStruct(r.shape, r.dtype) for r in results),
            in_specs=[pl.BlockSpec(memory_space=pl.ANY)] * 3,
            out_specs=(hbm,) * 3,
            scratch_shapes=[dma((3,))],
            compiler_params=pltpu.CompilerParams(vmem_limit_bytes=1024 * 1024),
        )(*results)

    return jax.shard_map(
        on_device,
        mesh=mesh,
        in_specs=(
            P("section", "seq", None),
            P("section", "seq", None),
            P("section", "seq", None),
            P("section", "seq", None),
            P("section", None),
            P("seq", None),
        ),
        out_specs=(P("section", "seq", None), P("section", "seq", None), P("section", "seq", None)),
        check_vma=False,
    )
```
